128 devices in a mesh: dp: 2 (over core), expert: 16 (over x, z), etp: 4 (over y).
Axes of the slice: x: 4, y: 4, z: 4, core: 2. Of those that a mesh axis runs over, the one named last changes fastest.
Arguments:
- master_old: float32 [16, 3584, 1024], P('expert', 'dp', 'etp'), may hold values from -6 to 6
- moment_old: float32 [16, 3584, 1024], P('expert', 'dp', 'etp'), may hold values from -6 to 6
- second_old: float32 [16, 3584, 1024], P('expert', 'dp', 'etp'), may hold values from 0.1 to 10
- grad_parts: bfloat16 [2, 32, 3584, 1024], P('dp', 'expert', None, 'etp'), may hold values from -384 to 384
- old_expert: int32 [16], replicated, may hold values from 0 to 15, as said below
- slot_expert: int32 [32], replicated, may hold values from -1 to 15, as said below
- owner_slot: int32 [16], replicated, may hold values from 0 to 31, as said below
- token_count: int32 [16], replicated, may hold values from 16 to 256
Outputs:
- master_new: float32 [32, 3584, 1024], P('expert', 'dp', 'etp')
- moment_new: float32 [32, 3584, 1024], P('expert', 'dp', 'etp')
- second_new: float32 [32, 3584, 1024], P('expert', 'dp', 'etp')
- slot_weights: bfloat16 [32, 3584, 1024], P('expert', None, 'etp')
The draws below stay inside these ranges and needn't reach their ends.
Inputs may be any that keep to these rules, and one draw needn't show every extreme that they name: `old_expert`: every expert is named exactly once. `slot_expert`: every expert is hosted by one or two slots, never twice on one device; 4 experts have two. Slots s and s + 1 for even s belong to one device. Each device owns 0 to 2 experts, and some device owns exactly 2. Slot 0 and the last slot are owner slots. owner_slot[e] is a slot s with slot_expert[s] = e; each slot owns at most one expert.
All inputs are finite; a program needn't handle non-finite values.
Results may differ from the reference program's by a relative error of at most 0.009.
Values may be sent and summed in bfloat16 or wider, within the bound.
A program may use at most 128 MiB of HBM per device.

```python
import math
import jax
import jax.numpy as jnp
from jax import lax

DW = 3584
FW = 1024
HOLD = 2
EXPERTS = 16
SLOTS = 32
REDUN = 4
N_DP = 2


def placement_tables(key):
    base = jax.random.fold_in(key, 41)
    key_dev, key_own, key_spare, key_flip = jax.random.split(base, 4)
    middle = jax.random.permutation(key_dev, EXPERTS - 2).astype(jnp.int32) + 2
    ranking = jnp.concatenate([jnp.ones((1,), jnp.int32), middle, jnp.zeros((1,), jnp.int32)]).astype(jnp.int32)
    flipped = jax.random.randint(key_flip, (EXPERTS,), 0, 2).astype(jnp.int32)
    flipped = flipped.at[0].set(0)
    within = jnp.arange(HOLD, dtype=jnp.int32)[None, :] ^ flipped[:, None]
    rank_col = ranking[:, None]
    owned = ((rank_col < REDUN) | (rank_col < EXPERTS - REDUN) & (within == 0)).reshape(-1)
    spare = ((rank_col >= EXPERTS - REDUN) & (within == 0)).reshape(-1)
    own_index = jnp.maximum(jnp.cumsum(owned.astype(jnp.int32)) - 1, 0)
    spare_index = jnp.maximum(jnp.cumsum(spare.astype(jnp.int32)) - 1, 0)
    owner_perm = jax.random.permutation(key_own, EXPERTS).astype(jnp.int32)
    spare_perm = jax.random.permutation(key_spare, EXPERTS).astype(jnp.int32)
    slot_table = jnp.where(owned, owner_perm[own_index], jnp.where(spare, spare_perm[spare_index], -1)).astype(jnp.int32)
    slot_ids = jnp.arange(SLOTS, dtype=jnp.int32)
    matching = owned[None, :] & (slot_table[None, :] == jnp.arange(EXPERTS, dtype=jnp.int32)[:, None])
    owner_table = jnp.sum(jnp.where(matching, slot_ids[None, :], 0), axis=1).astype(jnp.int32)
    return (slot_table, owner_table)


def draw_old_expert(key, part):
    mixed = jax.random.fold_in(jax.random.fold_in(key, 9173), 2711)
    scores = jax.random.randint(mixed, (EXPERTS,), 0, 1 << 20).astype(jnp.int32)
    scores = scores * 64 + jnp.arange(EXPERTS, dtype=jnp.int32)
    return jnp.argsort(scores, stable=True).astype(jnp.int32)


def draw_slot_expert(key, part):
    return placement_tables(key)[0]


def draw_owner_slot(key, part):
    return placement_tables(key)[1]


def set_ends(drawn, key, low, high):
    longest = drawn.shape.index(max(drawn.shape))
    spots = []
    for shift in (0, 1):
        where = [jax.random.randint(jax.random.fold_in(key, axis), (), 0, length) for axis, length in enumerate(drawn.shape)]
        where[longest] = (where[longest] + shift) % drawn.shape[longest]
        spots.append(tuple(where))
    return drawn.at[spots[0]].set(low).at[spots[1]].set(high)


def shard_levels(stream_key, shape, pieces, low, largest):
    loudness, own = 1.0, jax.random.fold_in(stream_key, 6)
    for dim, blocks in pieces:
        draws = jnp.exp(jax.random.uniform(jax.random.fold_in(own, dim), (blocks,), jnp.float32, low / len(pieces), largest / len(pieces)))
        loudness = loudness * jnp.repeat(draws, shape[dim] // blocks).reshape([-1 if axis == dim else 1 for axis in range(len(shape))])
    return loudness


def normal_values(key, dims, deviation, most, cuts=(), held_as=jnp.bfloat16):
    factor_of = shard_levels(key, dims, cuts, -0.22, 0.18) if cuts else 1.0
    values = jax.random.normal(key, dims, jnp.float32) * deviation * factor_of
    return jnp.minimum(jnp.maximum(values, -most), most).astype(held_as)


def setup_inputs(seed: int = 0) -> dict:
    key_list = jax.random.split(jax.random.key(seed), 9)
    master_old = normal_values(key_list[0], (EXPERTS, DW, FW), 1.0, 6.0, ((0, 16), (1, 2), (2, 4)), jnp.float32)
    moment_old = normal_values(key_list[1], (EXPERTS, DW, FW), 1.0, 6.0, ((0, 16), (1, 2), (2, 4)), jnp.float32)
    second_old = jnp.clip(jnp.exp(math.log(10.0) - 4.6051702 * jax.random.uniform(key_list[2], (EXPERTS, DW, FW), jnp.float32) ** shard_levels(key_list[2], (EXPERTS, DW, FW), ((0, 16), (1, 2), (2, 4)), -0.2, 0.2)), 0.1, 10.0)
    grad_parts = normal_values(key_list[3], (N_DP, SLOTS, DW, FW), 64.0, 384.0, ((0, 2), (1, 16), (3, 4)))
    old_expert = draw_old_expert(jax.random.fold_in(key_list[8], 71), 0)
    slot_expert = draw_slot_expert(jax.random.fold_in(key_list[8], 71), 0)
    owner_slot = draw_owner_slot(jax.random.fold_in(key_list[8], 71), 0)
    token_count = set_ends(jax.random.randint(key_list[7], (EXPERTS,), 16, 257), jax.random.fold_in(key_list[7], 1), 16, 256).astype(jnp.int32)
    return {"master_old": master_old, "moment_old": moment_old, "second_old": second_old, "grad_parts": grad_parts, "old_expert": old_expert, "slot_expert": slot_expert, "owner_slot": owner_slot, "token_count": token_count}


beta_one = 0.9
beta_two = 0.95
learn_rate = 0.05
decay_rate = 0.1
adam_eps = 1e-08

def adamw_update(gradient, master, moment, second):
    moment_next = beta_one * moment + (1.0 - beta_one) * gradient
    second_next = beta_two * second + (1.0 - beta_two) * gradient * gradient
    master_next = master - learn_rate * (moment_next / (jnp.sqrt(second_next) + adam_eps) + decay_rate * master)
    return (master_next, moment_next, second_next)

def reference(master_old, moment_old, second_old, grad_parts, old_expert, slot_expert, owner_slot, token_count):
    summed = lax.optimization_barrier(jnp.sum(grad_parts.astype(jnp.float32), axis=0))
    expert_total = master_old.shape[0]
    slot_total = summed.shape[0]
    expert_ids = jnp.arange(expert_total, dtype=jnp.int32)
    slot_ids = jnp.arange(slot_total, dtype=jnp.int32)
    chooser = (slot_expert[None, :] == expert_ids[:, None]).astype(jnp.float32)
    flattened = summed.reshape(slot_total, -1)
    gradient = jnp.dot(chooser, flattened, precision=lax.Precision.HIGHEST, preferred_element_type=jnp.float32)
    gradient = gradient.reshape(master_old.shape) / token_count.astype(jnp.float32)[:, None, None]
    inverse = jnp.zeros((expert_total,), jnp.int32).at[old_expert].set(expert_ids)
    master_prev = master_old[inverse]
    moment_prev = moment_old[inverse]
    second_prev = second_old[inverse]
    master_next, moment_next, second_next = adamw_update(gradient, master_prev, moment_prev, second_prev)
    safe_ids = jnp.maximum(slot_expert, 0).astype(jnp.int32)
    held_mask = slot_expert >= 0
    owned_mask = held_mask & (owner_slot[safe_ids] == slot_ids)
    zero_value = jnp.float32(0.0)
    master_new = jnp.where(owned_mask[:, None, None], master_next[safe_ids], zero_value)
    moment_new = jnp.where(owned_mask[:, None, None], moment_next[safe_ids], zero_value)
    second_new = jnp.where(owned_mask[:, None, None], second_next[safe_ids], zero_value)
    slot_weights = jnp.where(held_mask[:, None, None], master_next[safe_ids], zero_value).astype(jnp.bfloat16)
    return (master_new, moment_new, second_new, slot_weights)
```

```python
import functools

import jax
import jax.numpy as jnp
from jax import lax
from jax.experimental import pallas as pl
from jax.experimental.pallas import tpu as pltpu
from jax.sharding import PartitionSpec as P

beta_one = 0.9
beta_two = 0.95
learn_rate = 0.05
decay_rate = 0.1
adam_eps = 1e-08

MESH = pl.DeviceIdType.MESH
SIDE = 4
PEERS = SIDE * SIDE
FIELDS = 5
RESULTS = 6
PIECE = 16
ORDER = (
    (0, 1), (0, 3), (1, 0), (3, 0), (1, 1), (3, 3), (1, 3), (3, 1),
    (0, 2), (2, 0), (2, 1), (2, 3), (1, 2), (3, 2), (2, 2),
)


def exchange_kernel(
    chunks,
    old_ref, slot_ref, count_ref,
    master_ref, moment_ref, second_ref, grad_ref,
    out_ref, other_ref,
    *scratch,
):
    landed = scratch[:chunks]
    (states, grad_own, grad_other, packed, updated, table,
     load_sem, dp_send, dp_recv, send_one, recv_one, send_two, recv_two,
     fwd_send, fwd_recv) = scratch[chunks:]
    rows = states.shape[2]
    half = chunks * rows
    core = lax.axis_index("dp")
    me = lax.axis_index("expert")
    plane = lax.axis_index("etp")
    my_x = me // SIDE
    my_z = me % SIDE
    partner = (1 - core, me, plane)
    targets = [
        lax.rem(my_x + dx, SIDE) * SIDE + lax.rem(my_z + dz, SIDE) for dx, dz in ORDER
    ]

    def loads(k):
        window = pl.ds(k * rows, rows)
        copies = [
            pltpu.make_async_copy(ref.at[0, window], states.at[k, a], load_sem.at[k, a])
            for a, ref in enumerate((master_ref, moment_ref, second_ref))
        ]
        copies.append(
            pltpu.make_async_copy(
                grad_ref.at[0, :, pl.ds(core * half + k * rows, rows)],
                grad_own.at[k],
                load_sem.at[k, 3],
            )
        )
        return copies

    def swap(k):
        return pltpu.make_async_remote_copy(
            src_ref=grad_ref.at[0, :, pl.ds((1 - core) * half + k * rows, rows)],
            dst_ref=grad_other.at[k],
            send_sem=dp_send.at[k],
            recv_sem=dp_recv.at[k],
            device_id=partner,
            device_id_type=MESH,
        )

    def scatter(k):
        for other in targets:
            pltpu.make_async_remote_copy(
                src_ref=packed.at[k, other],
                dst_ref=landed[k].at[pl.ds(me * FIELDS, FIELDS)],
                send_sem=send_one.at[k],
                recv_sem=recv_one.at[k],
                device_id=(core, other, plane),
                device_id_type=MESH,
            ).start()
        pltpu.make_async_copy(
            packed.at[k, me], landed[k].at[pl.ds(me * FIELDS, FIELDS)], recv_one.at[k]
        ).start()

    def deliver(k):
        window = pl.ds(k * rows + me * PIECE, PIECE)
        for other in targets:
            pltpu.make_async_remote_copy(
                src_ref=updated.at[k, other],
                dst_ref=out_ref.at[:, window],
                send_sem=send_two.at[k],
                recv_sem=recv_two.at[k],
                device_id=(core, other, plane),
                device_id_type=MESH,
            ).start()
        pltpu.make_async_copy(
            updated.at[k, me], out_ref.at[:, window], recv_two.at[k]
        ).start()

    def pack(k):
        for copy in loads(k):
            copy.wait()
        swap(k).wait_recv()

        def body(i, carry):
            window = pl.ds(pl.multiple_of(i * PIECE, PIECE), PIECE)
            for a in range(3):
                packed[k, i, a] = states[k, a, window].astype(jnp.bfloat16)
            for h in range(2):
                packed[k, i, 3 + h] = (
                    grad_own[k, h, window].astype(jnp.float32)
                    + grad_other[k, h, window].astype(jnp.float32)
                ).astype(jnp.bfloat16)
            return carry

        lax.fori_loop(0, PEERS, body, 0)

    def update(k):
        source = landed[k]

        def body(d, carry):
            for h in range(2):
                s = 2 * d + h
                state = table[0, s]
                first = table[1, s]
                last = table[2, s]
                twice = table[3, s].astype(jnp.float32)
                scale = 1.0 / jnp.full((PIECE, 256), table[4, s].astype(jnp.float32))
                gradient = (
                    source[first].astype(jnp.float32)
                    + twice * source[last].astype(jnp.float32)
                ) * scale
                master = source[state].astype(jnp.float32)
                moment = source[state + 1].astype(jnp.float32)
                second = source[state + 2].astype(jnp.float32)
                moment = beta_one * moment + (1.0 - beta_one) * gradient
                second = beta_two * second + (1.0 - beta_two) * gradient * gradient
                master = master - learn_rate * (
                    moment / (jnp.sqrt(second) + adam_eps) + decay_rate * master
                )
                updated[k, d, h] = master.astype(jnp.bfloat16)
                updated[k, d, 2 + h] = moment.astype(jnp.bfloat16)
                updated[k, d, 4 + h] = second.astype(jnp.bfloat16)
            return carry

        lax.fori_loop(0, PEERS, body, 0)

    def forward(k):
        window = pl.ds(k * rows, rows)
        return pltpu.make_async_remote_copy(
            src_ref=out_ref.at[pl.ds(0, 2), window],
            dst_ref=other_ref.at[:, window],
            send_sem=fwd_send.at[k],
            recv_sem=fwd_recv.at[k],
            device_id=partner,
            device_id_type=MESH,
        )

    def all_bytes(ref, sem):
        pltpu.make_async_copy(ref, ref, sem).wait()

    for k in range(chunks):
        for copy in loads(k):
            copy.start()

    barrier = pltpu.get_barrier_semaphore()
    for other in targets:
        pl.semaphore_signal(
            barrier, inc=1, device_id=(core, other, plane), device_id_type=MESH
        )
    pl.semaphore_signal(barrier, inc=1, device_id=partner, device_id_type=MESH)
    pl.semaphore_wait(barrier, PEERS)

    for k in range(chunks):
        swap(k).start()

    def fill_table(s, carry):
        expert = jnp.maximum(slot_ref[s], 0)
        holder = jnp.int32(0)
        for j in range(PEERS):
            holder = jnp.where(old_ref[j] == expert, j, holder)
        first = jnp.int32(0)
        last = jnp.int32(0)
        for t in range(2 * PEERS):
            last = jnp.where(slot_ref[t] == expert, t, last)
            back = 2 * PEERS - 1 - t
            first = jnp.where(slot_ref[back] == expert, back, first)
        table[0, s] = holder * FIELDS
        table[1, s] = (first // 2) * FIELDS + 3 + first % 2
        table[2, s] = (last // 2) * FIELDS + 3 + last % 2
        table[3, s] = jnp.where(first == last, 0, 1)
        table[4, s] = count_ref[expert]
        return carry

    pack(0)
    scatter(0)
    pack(1)
    scatter(1)
    lax.fori_loop(0, 2 * PEERS, fill_table, 0)
    for k in range(chunks):
        all_bytes(landed[k], recv_one.at[k])
        update(k)
        deliver(k)
        if k + 2 < chunks:
            pack(k + 2)
            scatter(k + 2)
    for k in range(chunks):
        all_bytes(out_ref.at[:, pl.ds(k * rows, rows)], recv_two.at[k])
        forward(k).start()
    for k in range(chunks):
        swap(k).wait_send()
        all_bytes(packed.at[k, pl.ds(0, PEERS - 1)], send_one.at[k])
        all_bytes(updated.at[k, pl.ds(0, PEERS - 1)], send_two.at[k])
    for k in range(chunks):
        forward(k).wait()


def expand_kernel(slot_ref, owner_ref, here_ref, there_ref, master_ref, moment_ref, second_ref, weight_ref):
    core = lax.axis_index("dp")
    me = lax.axis_index("expert")
    for h in range(2):
        slot = 2 * me + h
        expert = slot_ref[slot]
        held = expert >= 0
        owned = held & (owner_ref[jnp.maximum(expert, 0)] == slot)
        master = here_ref[h]
        for ref, field in ((master_ref, 0), (moment_ref, 2), (second_ref, 4)):
            value = here_ref[field + h].astype(jnp.float32)
            ref[h] = jnp.where(owned, value, 0.0)
        here = jnp.where(held, master.astype(jnp.float32), 0.0).astype(jnp.bfloat16)
        there = jnp.where(held, there_ref[h].astype(jnp.float32), 0.0).astype(jnp.bfloat16)
        weight_ref[h, core] = here
        weight_ref[h, 1 - core] = there


def per_device(
    master_old, moment_old, second_old, grad_parts, old_expert, slot_expert, owner_slot, token_count
):
    half, width = master_old.shape[1:]
    rows = PEERS * PIECE
    chunks = half // rows
    anywhere = pl.BlockSpec(memory_space=pl.ANY)
    scalars = pl.BlockSpec(memory_space=pltpu.SMEM)
    bf16 = jnp.bfloat16
    dma = pltpu.SemaphoreType.DMA
    here, there = pl.pallas_call(
        functools.partial(exchange_kernel, chunks),
        out_shape=(
            jax.ShapeDtypeStruct((RESULTS, half, width), bf16),
            jax.ShapeDtypeStruct((2, half, width), bf16),
        ),
        in_specs=[scalars] * 3 + [anywhere] * 4,
        out_specs=(anywhere, anywhere),
        scratch_shapes=[pltpu.VMEM((PEERS * FIELDS, PIECE, width), bf16)] * chunks
        + [
            pltpu.VMEM((chunks, 3, rows, width), jnp.float32),
            pltpu.VMEM((chunks, 2, rows, width), bf16),
            pltpu.VMEM((chunks, 2, rows, width), bf16),
            pltpu.VMEM((chunks, PEERS, FIELDS, PIECE, width), bf16),
            pltpu.VMEM((chunks, PEERS, RESULTS, PIECE, width), bf16),
            pltpu.SMEM((5, 2 * PEERS), jnp.int32),
            dma((chunks, 4)),
        ]
        + [dma((chunks,))] * 8,
        compiler_params=pltpu.CompilerParams(collective_id=0, has_side_effects=True),
        name="exchange",
    )(old_expert, slot_expert, token_count, master_old, moment_old, second_old, grad_parts)

    block = 256
    wide = jax.ShapeDtypeStruct((2, half, width), jnp.float32)
    state_spec = pl.BlockSpec((2, block, width), lambda i: (0, i, 0))
    master_new, moment_new, second_new, weights = pl.pallas_call(
        expand_kernel,
        out_shape=(wide, wide, wide, jax.ShapeDtypeStruct((2, 2, half, width), bf16)),
        grid=(half // block,),
        in_specs=[
            scalars,
            scalars,
            pl.BlockSpec((RESULTS, block, width), lambda i: (0, i, 0)),
            state_spec,
        ],
        out_specs=(
            state_spec,
            state_spec,
            state_spec,
            pl.BlockSpec((2, 2, block, width), lambda i: (0, 0, i, 0)),
        ),
        name="expand",
    )(slot_expert, owner_slot, here, there)
    return (master_new, moment_new, second_new, weights.reshape(2, 2 * half, width))


def solution(mesh):
    placed = (
        P("expert", "dp", "etp"),
        P("expert", "dp", "etp"),
        P("expert", "dp", "etp"),
        P("dp", "expert", None, "etp"),
        P(),
        P(),
        P(),
        P(),
    )
    return jax.shard_map(
        per_device,
        mesh=mesh,
        in_specs=placed,
        out_specs=(
            P("expert", "dp", "etp"),
            P("expert", "dp", "etp"),
            P("expert", "dp", "etp"),
            P("expert", None, "etp"),
        ),
        check_vma=False,
    )
```

```python
import functools

import jax
import jax.numpy as jnp
from jax import lax
from jax.experimental import pallas as pl
from jax.experimental.pallas import tpu as pltpu
from jax.sharding import PartitionSpec as P

beta_one = 0.9
beta_two = 0.95
learn_rate = 0.05
decay_rate = 0.1
adam_eps = 1e-08

MESH = pl.DeviceIdType.MESH
SIDE = 4
PEERS = SIDE * SIDE
FIELDS = 5
RESULTS = 6
PIECE = 16
ORDER = (
    (0, 1), (0, 3), (1, 0), (3, 0), (1, 1), (3, 3), (1, 3), (3, 1),
    (0, 2), (2, 0), (2, 1), (2, 3), (1, 2), (3, 2), (2, 2),
)


def exchange_kernel(
    chunks,
    old_hbm, slot_hbm, owner_hbm, count_hbm,
    master_ref, moment_ref, second_ref, grad_ref,
    out_ref, other_ref,
    *scratch,
):
    landed = scratch[:chunks]
    (states, grad_own, grad_other, packed, updated, table,
     old_ref, slot_ref, owner_ref, count_ref, table_sem,
     load_sem, dp_send, dp_recv, send_one, recv_one, send_two, recv_two,
     fwd_send, fwd_recv) = scratch[chunks:]
    tables = [
        pltpu.make_async_copy(source, held, table_sem.at[n])
        for n, (source, held) in enumerate(
            ((old_hbm, old_ref), (slot_hbm, slot_ref), (owner_hbm, owner_ref), (count_hbm, count_ref))
        )
    ]
    rows = states.shape[2]
    half = chunks * rows
    core = lax.axis_index("dp")
    me = lax.axis_index("expert")
    plane = lax.axis_index("etp")
    my_x = me // SIDE
    my_z = me % SIDE
    partner = (1 - core, me, plane)
    targets = [
        lax.rem(my_x + dx, SIDE) * SIDE + lax.rem(my_z + dz, SIDE) for dx, dz in ORDER
    ]

    def load_states(k):
        window = pl.ds(k * rows, rows)
        return [
            pltpu.make_async_copy(ref.at[0, window], states.at[k, a], load_sem.at[k, a])
            for a, ref in enumerate((master_ref, moment_ref, second_ref))
        ]

    def load_grads(k):
        return pltpu.make_async_copy(
            grad_ref.at[0, :, pl.ds(core * half + k * rows, rows)],
            grad_own.at[k],
            load_sem.at[k, 3],
        )

    def swap(k):
        return pltpu.make_async_remote_copy(
            src_ref=grad_ref.at[0, :, pl.ds((1 - core) * half + k * rows, rows)],
            dst_ref=grad_other.at[k],
            send_sem=dp_send.at[k],
            recv_sem=dp_recv.at[k],
            device_id=partner,
            device_id_type=MESH,
        )

    def spread(source, target, send, recv):
        for other in targets:
            pltpu.make_async_remote_copy(
                src_ref=source(other),
                dst_ref=target,
                send_sem=send,
                recv_sem=recv,
                device_id=(core, other, plane),
                device_id_type=MESH,
            ).start()
        pltpu.make_async_copy(source(me), target, recv).start()

    def scatter(k, first, count):
        spread(
            lambda i: packed.at[k, i, pl.ds(first, count)],
            landed[k].at[pl.ds(me * FIELDS + first, count)],
            send_one.at[k],
            recv_one.at[k],
        )

    def deliver(k, first, count, part):
        window = pl.ds(k * rows + me * PIECE, PIECE)
        spread(
            lambda i: updated.at[k, i, pl.ds(first, count)],
            out_ref.at[pl.ds(first, count), window],
            send_two.at[k],
            recv_two.at[k, part],
        )

    def pack_states(k):
        for copy in load_states(k):
            copy.wait()

        def body(i, carry):
            window = pl.ds(pl.multiple_of(i * PIECE, PIECE), PIECE)
            for a in range(3):
                packed[k, i, a] = states[k, a, window].astype(jnp.bfloat16)
            return carry

        lax.fori_loop(0, PEERS, body, 0)

    def pack_grads(k):
        load_grads(k).wait()
        swap(k).wait_recv()

        def body(i, carry):
            window = pl.ds(pl.multiple_of(i * PIECE, PIECE), PIECE)
            for h in range(2):
                packed[k, i, 3 + h] = (
                    grad_own[k, h, window].astype(jnp.float32)
                    + grad_other[k, h, window].astype(jnp.float32)
                ).astype(jnp.bfloat16)
            return carry

        lax.fori_loop(0, PEERS, body, 0)

    def update(k):
        source = landed[k]

        def body(d, carry):
            for h in range(2):
                s = 2 * d + h
                state = table[0, s]
                first = table[1, s]
                last = table[2, s]
                twice = table[3, s].astype(jnp.float32)
                scale = 1.0 / jnp.full((PIECE, 256), table[4, s].astype(jnp.float32))
                gradient = (
                    source[first].astype(jnp.float32)
                    + twice * source[last].astype(jnp.float32)
                ) * scale
                master = source[state].astype(jnp.float32)
                moment = source[state + 1].astype(jnp.float32)
                second = source[state + 2].astype(jnp.float32)
                moment = beta_one * moment + (1.0 - beta_one) * gradient
                second = beta_two * second + (1.0 - beta_two) * gradient * gradient
                master = master - learn_rate * (
                    moment / (jnp.sqrt(second) + adam_eps) + decay_rate * master
                )
                held = table[5, s] > 0
                owned = table[6, s] > 0
                updated[k, d, h] = jnp.where(held, master, 0.0).astype(jnp.bfloat16)
                updated[k, d, 2 + h] = jnp.where(owned, moment, 0.0).astype(jnp.bfloat16)
                updated[k, d, 4 + h] = jnp.where(owned, second, 0.0).astype(jnp.bfloat16)
            return carry

        lax.fori_loop(0, PEERS, body, 0)

    def forward(k):
        window = pl.ds(k * rows, rows)
        return pltpu.make_async_remote_copy(
            src_ref=out_ref.at[pl.ds(0, 2), window],
            dst_ref=other_ref.at[:, window],
            send_sem=fwd_send.at[k],
            recv_sem=fwd_recv.at[k],
            device_id=partner,
            device_id_type=MESH,
        )

    def all_bytes(ref, sem):
        pltpu.make_async_copy(ref, ref, sem).wait()

    for copy in tables:
        copy.start()
    for k in range(chunks):
        for copy in load_states(k) + [load_grads(k)]:
            copy.start()

    barrier = pltpu.get_barrier_semaphore()
    for other in targets:
        pl.semaphore_signal(
            barrier, inc=1, device_id=(core, other, plane), device_id_type=MESH
        )
    pl.semaphore_signal(barrier, inc=1, device_id=partner, device_id_type=MESH)
    pack_states(0)
    pl.semaphore_wait(barrier, PEERS)

    for k in range(chunks):
        swap(k).start()

    def fill_table(s, carry):
        expert = jnp.maximum(slot_ref[s], 0)
        holder = jnp.int32(0)
        for j in range(PEERS):
            holder = jnp.where(old_ref[j] == expert, j, holder)
        first = jnp.int32(0)
        last = jnp.int32(0)
        for t in range(2 * PEERS):
            last = jnp.where(slot_ref[t] == expert, t, last)
            back = 2 * PEERS - 1 - t
            first = jnp.where(slot_ref[back] == expert, back, first)
        table[0, s] = holder * FIELDS
        table[1, s] = (first // 2) * FIELDS + 3 + first % 2
        table[2, s] = (last // 2) * FIELDS + 3 + last % 2
        table[3, s] = jnp.where(first == last, 0, 1)
        table[4, s] = count_ref[expert]
        table[5, s] = jnp.where(slot_ref[s] >= 0, 1, 0)
        table[6, s] = jnp.where((slot_ref[s] >= 0) & (owner_ref[expert] == s), 1, 0)
        return carry

    scatter(0, 0, 3)
    pack_grads(0)
    scatter(0, 3, 2)
    pack_states(1)
    pack_grads(1)
    scatter(1, 0, FIELDS)
    for copy in tables:
        copy.wait()
    lax.fori_loop(0, 2 * PEERS, fill_table, 0)
    final = chunks - 1
    for k in range(chunks):
        all_bytes(landed[k], recv_one.at[k])
        update(k)
        if k < final:
            deliver(k, 0, RESULTS, 0)
        else:
            deliver(k, 0, 2, 0)
            deliver(k, 2, 4, 1)
        if k + 2 < chunks:
            pack_states(k + 2)
            pack_grads(k + 2)
            scatter(k + 2, 0, FIELDS)
    for k in range(chunks):
        fields = pl.ds(0, RESULTS if k < final else 2)
        all_bytes(out_ref.at[fields, pl.ds(k * rows, rows)], recv_two.at[k, 0])
        forward(k).start()
    all_bytes(out_ref.at[pl.ds(2, 4), pl.ds(final * rows, rows)], recv_two.at[final, 1])
    for k in range(chunks):
        swap(k).wait_send()
        all_bytes(packed.at[k, pl.ds(0, PEERS - 1)], send_one.at[k])
        all_bytes(updated.at[k, pl.ds(0, PEERS - 1)], send_two.at[k])
    for k in range(chunks):
        forward(k).wait()


def expand_kernel(
    slot_hbm, owner_hbm, here_ref, there_ref,
    master_ref, moment_ref, second_ref, weight_ref,
    wide, slot_ref, owner_ref, sems, weight_sems, table_sems,
):
    core = lax.axis_index("dp")
    me = lax.axis_index("expert")
    half = here_ref.shape[1]
    steps, rows = wide.shape[1], wide.shape[3]
    outs = (master_ref, moment_ref, second_ref)
    weights = [
        pltpu.make_async_copy(
            here_ref.at[pl.ds(0, 2)], weight_ref.at[:, pl.ds(core * half, half)], weight_sems.at[0]
        ),
        pltpu.make_async_copy(
            there_ref, weight_ref.at[:, pl.ds((1 - core) * half, half)], weight_sems.at[1]
        ),
    ]

    def store(a, k):
        return pltpu.make_async_copy(
            wide.at[a, k], outs[a].at[:, pl.ds(k * rows, rows)], sems.at[a, k]
        )

    tables = [
        pltpu.make_async_copy(slot_hbm, slot_ref, table_sems.at[0]),
        pltpu.make_async_copy(owner_hbm, owner_ref, table_sems.at[1]),
    ]
    for copy in tables + weights:
        copy.start()
    for a in (1, 2):
        for k in range(steps):
            for h in range(2):
                wide[a, k, h] = here_ref[2 * a + h, pl.ds(k * rows, rows)].astype(jnp.float32)
            store(a, k).start()
    for copy in tables:
        copy.wait()
    owned = []
    for h in range(2):
        slot = 2 * me + h
        expert = slot_ref[slot]
        owned.append((expert >= 0) & (owner_ref[jnp.maximum(expert, 0)] == slot))
    for k in range(steps):
        for h in range(2):
            value = here_ref[h, pl.ds(k * rows, rows)].astype(jnp.float32)
            wide[0, k, h] = jnp.where(owned[h], value, 0.0)
        store(0, k).start()
    for copy in weights:
        copy.wait()
    for k in range(steps):
        for a in range(3):
            store(a, k).wait()


def per_device(
    master_old, moment_old, second_old, grad_parts, old_expert, slot_expert, owner_slot, token_count
):
    half, width = master_old.shape[1:]
    rows = PEERS * PIECE
    chunks = half // rows
    anywhere = pl.BlockSpec(memory_space=pl.ANY)
    vmem = pl.BlockSpec(memory_space=pltpu.VMEM)
    bf16 = jnp.bfloat16
    dma = pltpu.SemaphoreType.DMA
    here, there = pl.pallas_call(
        functools.partial(exchange_kernel, chunks),
        out_shape=(
            pltpu.VMEM((RESULTS, half, width), bf16),
            pltpu.VMEM((2, half, width), bf16),
        ),
        in_specs=[anywhere] * 8,
        out_specs=(vmem, vmem),
        scratch_shapes=[pltpu.VMEM((PEERS * FIELDS, PIECE, width), bf16)] * chunks
        + [
            pltpu.VMEM((chunks, 3, rows, width), jnp.float32),
            pltpu.VMEM((chunks, 2, rows, width), bf16),
            pltpu.VMEM((chunks, 2, rows, width), bf16),
            pltpu.VMEM((chunks, PEERS, FIELDS, PIECE, width), bf16),
            pltpu.VMEM((chunks, PEERS, RESULTS, PIECE, width), bf16),
            pltpu.SMEM((7, 2 * PEERS), jnp.int32),
            pltpu.SMEM(old_expert.shape, jnp.int32),
            pltpu.SMEM(slot_expert.shape, jnp.int32),
            pltpu.SMEM(owner_slot.shape, jnp.int32),
            pltpu.SMEM(token_count.shape, jnp.int32),
            dma((4,)),
            dma((chunks, 4)),
            dma((chunks,)),
            dma((chunks,)),
            dma((chunks,)),
            dma((chunks,)),
            dma((chunks,)),
            dma((chunks, 2)),
            dma((chunks,)),
            dma((chunks,)),
        ],
        compiler_params=pltpu.CompilerParams(
            collective_id=0, has_side_effects=True, vmem_limit_bytes=40 << 20
        ),
        name="exchange",
    )(
        *(
            pltpu.with_memory_space_constraint(a, pltpu.HBM)
            for a in (
                old_expert, slot_expert, owner_slot, token_count,
                master_old, moment_old, second_old, grad_parts,
            )
        ),
    )

    steps = 7
    wide = jax.ShapeDtypeStruct((2, half, width), jnp.float32)
    return pl.pallas_call(
        expand_kernel,
        out_shape=(wide, wide, wide, jax.ShapeDtypeStruct((2, 2 * half, width), bf16)),
        in_specs=[anywhere, anywhere, vmem, vmem],
        out_specs=(anywhere,) * 4,
        scratch_shapes=[
            pltpu.VMEM((3, steps, 2, half // steps, width), jnp.float32),
            pltpu.SMEM(slot_expert.shape, jnp.int32),
            pltpu.SMEM(owner_slot.shape, jnp.int32),
            dma((3, steps)),
            dma((2,)),
            dma((2,)),
        ],
        compiler_params=pltpu.CompilerParams(vmem_limit_bytes=24 << 20),
        name="expand",
    )(
        pltpu.with_memory_space_constraint(slot_expert, pltpu.HBM),
        pltpu.with_memory_space_constraint(owner_slot, pltpu.HBM),
        here,
        there,
    )


def solution(mesh):
    placed = (
        P("expert", "dp", "etp"),
        P("expert", "dp", "etp"),
        P("expert", "dp", "etp"),
        P("dp", "expert", None, "etp"),
        P(),
        P(),
        P(),
        P(),
    )
    return jax.shard_map(
        per_device,
        mesh=mesh,
        in_specs=placed,
        out_specs=(
            P("expert", "dp", "etp"),
            P("expert", "dp", "etp"),
            P("expert", "dp", "etp"),
            P("expert", None, "etp"),
        ),
        check_vma=False,
    )
```

```python
import functools

import jax
import jax.numpy as jnp
from jax import lax
from jax.experimental import pallas as pl
from jax.experimental.pallas import tpu as pltpu
from jax.sharding import PartitionSpec as P

beta_one = 0.9
beta_two = 0.95
learn_rate = 0.05
decay_rate = 0.1
adam_eps = 1e-08

MESH = pl.DeviceIdType.MESH
SIDE = 4
PEERS = SIDE * SIDE
FIELDS = 5
RESULTS = 6
PIECE = 16
ORDER = (
    (0, 1), (0, 3), (1, 0), (3, 0), (1, 1), (3, 3), (1, 3), (3, 1),
    (0, 2), (2, 0), (2, 1), (2, 3), (1, 2), (3, 2), (2, 2),
)


def exchange_kernel(
    chunks,
    old_hbm, slot_hbm, owner_hbm, count_hbm,
    master_ref, moment_ref, second_ref, grad_ref,
    out_ref, other_ref,
    *scratch,
):
    landed = scratch[:chunks]
    (states, grad_own, grad_other, packed, updated, table,
     old_ref, slot_ref, owner_ref, count_ref, table_sem,
     load_sem, dp_send, dp_recv, send_one, recv_one, send_two, recv_two,
     fwd_send, fwd_recv) = scratch[chunks:]
    tables = [
        pltpu.make_async_copy(source, held, table_sem.at[n])
        for n, (source, held) in enumerate(
            ((old_hbm, old_ref), (slot_hbm, slot_ref), (owner_hbm, owner_ref), (count_hbm, count_ref))
        )
    ]
    rows = states.shape[2]
    half = chunks * rows
    core = lax.axis_index("dp")
    me = lax.axis_index("expert")
    plane = lax.axis_index("etp")
    my_x = me // SIDE
    my_z = me % SIDE
    partner = (1 - core, me, plane)
    targets = [
        lax.rem(my_x + dx, SIDE) * SIDE + lax.rem(my_z + dz, SIDE) for dx, dz in ORDER
    ]

    def load_states(k):
        window = pl.ds(k * rows, rows)
        return [
            pltpu.make_async_copy(ref.at[0, window], states.at[k, a], load_sem.at[k, a])
            for a, ref in enumerate((master_ref, moment_ref, second_ref))
        ]

    def load_grads(k):
        return pltpu.make_async_copy(
            grad_ref.at[0, :, pl.ds(core * half + k * rows, rows)],
            grad_own.at[k],
            load_sem.at[k, 3],
        )

    def swap(k):
        return pltpu.make_async_remote_copy(
            src_ref=grad_ref.at[0, :, pl.ds((1 - core) * half + k * rows, rows)],
            dst_ref=grad_other.at[k],
            send_sem=dp_send.at[k],
            recv_sem=dp_recv.at[k],
            device_id=partner,
            device_id_type=MESH,
        )

    def spread(source, target, send, recv):
        for other in targets:
            pltpu.make_async_remote_copy(
                src_ref=source(other),
                dst_ref=target,
                send_sem=send,
                recv_sem=recv,
                device_id=(core, other, plane),
                device_id_type=MESH,
            ).start()
        pltpu.make_async_copy(source(me), target, recv).start()

    def scatter(k, first, count):
        spread(
            lambda i: packed.at[k, i, pl.ds(first, count)],
            landed[k].at[pl.ds(me * FIELDS + first, count)],
            send_one.at[k],
            recv_one.at[k],
        )

    def deliver(k, first, count, part):
        window = pl.ds(k * rows + me * PIECE, PIECE)
        spread(
            lambda i: updated.at[k, i, pl.ds(first, count)],
            out_ref.at[pl.ds(first, count), window],
            send_two.at[k],
            recv_two.at[k, part],
        )

    def pack_states(k):
        for copy in load_states(k):
            copy.wait()

        def body(i, carry):
            window = pl.ds(pl.multiple_of(i * PIECE, PIECE), PIECE)
            for a in range(3):
                packed[k, i, a] = states[k, a, window].astype(jnp.bfloat16)
            return carry

        lax.fori_loop(0, PEERS, body, 0)

    def pack_grads(k):
        load_grads(k).wait()
        swap(k).wait_recv()

        def body(i, carry):
            window = pl.ds(pl.multiple_of(i * PIECE, PIECE), PIECE)
            for h in range(2):
                packed[k, i, 3 + h] = (
                    grad_own[k, h, window].astype(jnp.float32)
                    + grad_other[k, h, window].astype(jnp.float32)
                ).astype(jnp.bfloat16)
            return carry

        lax.fori_loop(0, PEERS, body, 0)

    def update(k):
        source = landed[k]

        def body(d, carry):
            for h in range(2):
                s = 2 * d + h
                state = table[0, s]
                first = table[1, s]
                last = table[2, s]
                twice = table[3, s].astype(jnp.float32)
                scale = 1.0 / jnp.full((PIECE, 256), table[4, s].astype(jnp.float32))
                gradient = (
                    source[first].astype(jnp.float32)
                    + twice * source[last].astype(jnp.float32)
                ) * scale
                master = source[state].astype(jnp.float32)
                moment = source[state + 1].astype(jnp.float32)
                second = source[state + 2].astype(jnp.float32)
                moment = beta_one * moment + (1.0 - beta_one) * gradient
                second = beta_two * second + (1.0 - beta_two) * gradient * gradient
                master = master - learn_rate * (
                    moment / (jnp.sqrt(second) + adam_eps) + decay_rate * master
                )
                held = table[5, s] > 0
                owned = table[6, s] > 0
                updated[k, d, h] = jnp.where(held, master, 0.0).astype(jnp.bfloat16)
                updated[k, d, 2 + h] = jnp.where(owned, moment, 0.0).astype(jnp.bfloat16)
                updated[k, d, 4 + h] = jnp.where(owned, second, 0.0).astype(jnp.bfloat16)
            return carry

        lax.fori_loop(0, PEERS, body, 0)

    def forward(k):
        window = pl.ds(k * rows, rows)
        return pltpu.make_async_remote_copy(
            src_ref=out_ref.at[pl.ds(0, 2), window],
            dst_ref=other_ref.at[:, window],
            send_sem=fwd_send.at[k],
            recv_sem=fwd_recv.at[k],
            device_id=partner,
            device_id_type=MESH,
        )

    def all_bytes(ref, sem):
        pltpu.make_async_copy(ref, ref, sem).wait()

    for copy in tables:
        copy.start()
    for k in range(chunks):
        for copy in load_states(k) + [load_grads(k)]:
            copy.start()

    barrier = pltpu.get_barrier_semaphore()
    for other in targets:
        pl.semaphore_signal(
            barrier, inc=1, device_id=(core, other, plane), device_id_type=MESH
        )
    pl.semaphore_signal(barrier, inc=1, device_id=partner, device_id_type=MESH)
    pack_states(0)
    pl.semaphore_wait(barrier, PEERS)

    for k in range(chunks):
        swap(k).start()

    def fill_table(s, carry):
        expert = jnp.maximum(slot_ref[s], 0)
        holder = jnp.int32(0)
        for j in range(PEERS):
            holder = jnp.where(old_ref[j] == expert, j, holder)
        first = jnp.int32(0)
        last = jnp.int32(0)
        for t in range(2 * PEERS):
            last = jnp.where(slot_ref[t] == expert, t, last)
            back = 2 * PEERS - 1 - t
            first = jnp.where(slot_ref[back] == expert, back, first)
        table[0, s] = holder * FIELDS
        table[1, s] = (first // 2) * FIELDS + 3 + first % 2
        table[2, s] = (last // 2) * FIELDS + 3 + last % 2
        table[3, s] = jnp.where(first == last, 0, 1)
        table[4, s] = count_ref[expert]
        table[5, s] = jnp.where(slot_ref[s] >= 0, 1, 0)
        table[6, s] = jnp.where((slot_ref[s] >= 0) & (owner_ref[expert] == s), 1, 0)
        return carry

    scatter(0, 0, 3)
    pack_grads(0)
    scatter(0, 3, 2)
    pack_states(1)
    pack_grads(1)
    scatter(1, 0, FIELDS)
    for copy in tables:
        copy.wait()
    lax.fori_loop(0, 2 * PEERS, fill_table, 0)
    final = chunks - 1
    for k in range(chunks):
        all_bytes(landed[k], recv_one.at[k])
        update(k)
        if k < final:
            deliver(k, 0, RESULTS, 0)
        else:
            deliver(k, 0, 2, 0)
            deliver(k, 2, 4, 1)
        if k + 2 < chunks:
            pack_states(k + 2)
            pack_grads(k + 2)
            scatter(k + 2, 0, FIELDS)
    for k in range(chunks):
        fields = pl.ds(0, RESULTS if k < final else 2)
        all_bytes(out_ref.at[fields, pl.ds(k * rows, rows)], recv_two.at[k, 0])
        forward(k).start()
    all_bytes(out_ref.at[pl.ds(2, 4), pl.ds(final * rows, rows)], recv_two.at[final, 1])
    for k in range(chunks):
        swap(k).wait_send()
        all_bytes(packed.at[k, pl.ds(0, PEERS - 1)], send_one.at[k])
        all_bytes(updated.at[k, pl.ds(0, PEERS - 1)], send_two.at[k])
    for k in range(chunks):
        forward(k).wait()


def expand_kernel(
    slot_hbm, owner_hbm, here_ref, there_ref,
    master_ref, moment_ref, second_ref, weight_ref,
    wide, slot_ref, owner_ref, sems, weight_sems, table_sems,
):
    core = lax.axis_index("dp")
    me = lax.axis_index("expert")
    half = here_ref.shape[1]
    steps, rows = wide.shape[1], wide.shape[3]
    outs = (master_ref, moment_ref, second_ref)
    weights = [
        pltpu.make_async_copy(
            here_ref.at[pl.ds(0, 2)], weight_ref.at[:, pl.ds(core * half, half)], weight_sems.at[0]
        ),
        pltpu.make_async_copy(
            there_ref, weight_ref.at[:, pl.ds((1 - core) * half, half)], weight_sems.at[1]
        ),
    ]

    def store(a, k):
        return pltpu.make_async_copy(
            wide.at[a, k], outs[a].at[:, pl.ds(k * rows, rows)], sems.at[a, k]
        )

    tables = [
        pltpu.make_async_copy(slot_hbm, slot_ref, table_sems.at[0]),
        pltpu.make_async_copy(owner_hbm, owner_ref, table_sems.at[1]),
    ]
    for copy in tables + weights:
        copy.start()
    for a in (1, 2):
        for k in range(steps):
            for h in range(2):
                wide[a, k, h] = here_ref[2 * a + h, pl.ds(k * rows, rows)].astype(jnp.float32)
            store(a, k).start()
    for copy in tables:
        copy.wait()
    owned = []
    for h in range(2):
        slot = 2 * me + h
        expert = slot_ref[slot]
        owned.append((expert >= 0) & (owner_ref[jnp.maximum(expert, 0)] == slot))
    for k in range(steps):
        for h in range(2):
            value = here_ref[h, pl.ds(k * rows, rows)].astype(jnp.float32)
            wide[0, k, h] = jnp.where(owned[h], value, 0.0)
        store(0, k).start()
    for copy in weights:
        copy.wait()
    for k in range(steps):
        for a in range(3):
            store(a, k).wait()


def full_exchange(
    master_old, moment_old, second_old, grad_parts, old_expert, slot_expert, owner_slot, token_count
):
    half, width = master_old.shape[1:]
    rows = PEERS * PIECE
    chunks = half // rows
    anywhere = pl.BlockSpec(memory_space=pl.ANY)
    vmem = pl.BlockSpec(memory_space=pltpu.VMEM)
    bf16 = jnp.bfloat16
    dma = pltpu.SemaphoreType.DMA
    here, there = pl.pallas_call(
        functools.partial(exchange_kernel, chunks),
        out_shape=(
            pltpu.VMEM((RESULTS, half, width), bf16),
            pltpu.VMEM((2, half, width), bf16),
        ),
        in_specs=[anywhere] * 8,
        out_specs=(vmem, vmem),
        scratch_shapes=[pltpu.VMEM((PEERS * FIELDS, PIECE, width), bf16)] * chunks
        + [
            pltpu.VMEM((chunks, 3, rows, width), jnp.float32),
            pltpu.VMEM((chunks, 2, rows, width), bf16),
            pltpu.VMEM((chunks, 2, rows, width), bf16),
            pltpu.VMEM((chunks, PEERS, FIELDS, PIECE, width), bf16),
            pltpu.VMEM((chunks, PEERS, RESULTS, PIECE, width), bf16),
            pltpu.SMEM((7, 2 * PEERS), jnp.int32),
            pltpu.SMEM(old_expert.shape, jnp.int32),
            pltpu.SMEM(slot_expert.shape, jnp.int32),
            pltpu.SMEM(owner_slot.shape, jnp.int32),
            pltpu.SMEM(token_count.shape, jnp.int32),
            dma((4,)),
            dma((chunks, 4)),
            dma((chunks,)),
            dma((chunks,)),
            dma((chunks,)),
            dma((chunks,)),
            dma((chunks,)),
            dma((chunks, 2)),
            dma((chunks,)),
            dma((chunks,)),
        ],
        compiler_params=pltpu.CompilerParams(
            collective_id=0, has_side_effects=True, vmem_limit_bytes=40 << 20
        ),
        name="exchange",
    )(
        *(
            pltpu.with_memory_space_constraint(a, pltpu.HBM)
            for a in (
                old_expert, slot_expert, owner_slot, token_count,
                master_old, moment_old, second_old, grad_parts,
            )
        ),
    )

    steps = 7
    wide = jax.ShapeDtypeStruct((2, half, width), jnp.float32)
    return pl.pallas_call(
        expand_kernel,
        out_shape=(wide, wide, wide, jax.ShapeDtypeStruct((2, 2 * half, width), bf16)),
        in_specs=[anywhere, anywhere, vmem, vmem],
        out_specs=(anywhere,) * 4,
        scratch_shapes=[
            pltpu.VMEM((3, steps, 2, half // steps, width), jnp.float32),
            pltpu.SMEM(slot_expert.shape, jnp.int32),
            pltpu.SMEM(owner_slot.shape, jnp.int32),
            dma((3, steps)),
            dma((2,)),
            dma((2,)),
        ],
        compiler_params=pltpu.CompilerParams(vmem_limit_bytes=24 << 20),
        name="expand",
    )(
        pltpu.with_memory_space_constraint(slot_expert, pltpu.HBM),
        pltpu.with_memory_space_constraint(owner_slot, pltpu.HBM),
        here,
        there,
    )


LANES = 128
AHEAD = 4
KEEP = 2
SPREAD = 4


def line_device(h, p, q):
    return q * SIDE + p if h == 0 else p * SIDE + q


def short_kernel(
    chunks,
    old_hbm, slot_hbm, owner_hbm, count_hbm,
    master_ref, moment_ref, second_ref, grad_ref,
    one_ref, two_ref, other_one_ref, other_two_ref, flag_ref,
    *scratch,
):
    landed = scratch[:chunks]
    relay_grad = scratch[chunks : 2 * chunks]
    relay_two = scratch[2 * chunks : 3 * chunks]
    (states, grad_own, grad_other, packed, grad_line, grad_kept,
     update_one, update_two, two_line,
     old_ref, slot_ref, owner_ref, count_ref, both_t, rank_t, grad_t, device_t, entry_t, table_sem,
     load_sem, dp_send, dp_recv, spread_send, spread_recv, line_send, line_recv,
     one_send, one_recv, fwd_send, fwd_recv) = scratch[3 * chunks :]
    rows = states.shape[2]
    half = chunks * rows
    core = lax.axis_index("dp")
    me = lax.axis_index("expert")
    plane = lax.axis_index("etp")
    my_x = me // SIDE
    my_z = me % SIDE
    my_p = (my_z, my_x)
    my_q = (my_x, my_z)
    partner = (1 - core, me, plane)
    targets = [
        lax.rem(my_x + dx, SIDE) * SIDE + lax.rem(my_z + dz, SIDE) for dx, dz in ORDER
    ]
    tables = [
        pltpu.make_async_copy(source, held, table_sem.at[n])
        for n, (source, held) in enumerate(
            ((old_hbm, old_ref), (slot_hbm, slot_ref), (owner_hbm, owner_ref), (count_hbm, count_ref))
        )
    ]

    def load_states(k):
        window = pl.ds(k * rows, rows)
        return [
            pltpu.make_async_copy(ref.at[0, window], states.at[k, a], load_sem.at[k, a])
            for a, ref in enumerate((master_ref, moment_ref, second_ref))
        ]

    def load_grads(k):
        return pltpu.make_async_copy(
            grad_ref.at[0, :, pl.ds(core * half + k * rows, rows)],
            grad_own.at[k],
            load_sem.at[k, 3],
        )

    def swap(k):
        return pltpu.make_async_remote_copy(
            src_ref=grad_ref.at[0, :, pl.ds((1 - core) * half + k * rows, rows)],
            dst_ref=grad_other.at[k],
            send_sem=dp_send.at[k],
            recv_sem=dp_recv.at[k],
            device_id=partner,
            device_id_type=MESH,
        )

    def send(source, target, sems, other):
        pltpu.make_async_remote_copy(
            src_ref=source,
            dst_ref=target,
            send_sem=sems[0],
            recv_sem=sems[1],
            device_id=(core, other, plane),
            device_id_type=MESH,
        ).start()

    def spread(source, target, sems):
        for other in targets:
            send(source(other), target, sems, other)
        pltpu.make_async_copy(source(me), target, sems[1]).start()

    def along_line(use_p, source, target, sems):
        for step in (1, 3, 2):
            for h in range(2):
                if use_p:
                    place = lax.rem(my_p[h] + step, SIDE)
                    other = line_device(h, place, my_q[h])
                else:
                    place = lax.rem(my_q[h] + step, SIDE)
                    other = line_device(h, my_p[h], place)
                send(source(h, place), target(h), sems, other)
        for h in range(2):
            place = my_p[h] if use_p else my_q[h]
            pltpu.make_async_copy(source(h, place), target(h), sems[1]).start()

    def scatter(k, first, count):
        spread(
            lambda i: packed.at[k, i, pl.ds(first, count)],
            landed[k].at[pl.ds(me * SPREAD + first, count)],
            (spread_send.at[k], spread_recv.at[k]),
        )

    def scatter_second(k):
        along_line(
            False,
            lambda h, q: grad_line.at[k, h, q],
            lambda h: relay_grad[k].at[h, my_q[h]],
            (line_send.at[0, k], line_recv.at[0, k]),
        )

    def keep_grads(k):
        all_bytes(relay_grad[k], line_recv.at[0, k])
        for h in range(2):
            for r in range(KEEP):
                device = jnp.maximum(device_t[h, KEEP * my_p[h] + r], 0)
                q = device // SIDE if h == 0 else device % SIDE
                for p in range(SIDE):
                    grad_kept[k, h, p, r] = relay_grad[k][h, q, p]
        along_line(
            True,
            lambda h, p: grad_kept.at[k, h, p],
            lambda h: landed[k].at[pl.ds(PEERS * SPREAD + KEEP * my_p[h], KEEP), h],
            (line_send.at[1, k], line_recv.at[1, k]),
        )

    def fields_of(k):
        return ((0, 3),) if k < chunks - 1 else ((0, 1), (1, 2))

    def deliver_one(k):
        for part, (first, count) in enumerate(fields_of(k)):
            fields = pl.ds(first, count)
            spread(
                lambda i: update_one.at[k, i, fields],
                one_ref.at[fields, pl.ds(k * rows + me * PIECE, PIECE)],
                (one_send.at[k], one_recv.at[k, part]),
            )

    def deliver_two(k):
        along_line(
            True,
            lambda h, p: update_two.at[k, h, pl.ds(KEEP * p, KEEP)],
            lambda h: relay_two[k].at[h, my_p[h]],
            (line_send.at[2, k], line_recv.at[2, k]),
        )

    def pass_two(k):
        all_bytes(relay_two[k], line_recv.at[2, k])

        def body(q, carry):
            for h in range(2):
                r = rank_t[h, line_device(h, my_p[h], q)]
                for a in range(3):
                    for p in range(SIDE):
                        two_line[k, h, q, a, p] = relay_two[k][h, p, r, a]
            return carry

        lax.fori_loop(0, SIDE, body, 0)
        for part, (first, count) in enumerate(fields_of(k)):
            fields = pl.ds(first, count)
            along_line(
                False,
                lambda h, q: two_line.at[k, h, q, fields],
                lambda h: (
                    two_ref.at[k, 0, fields, my_q[0]]
                    if h == 0
                    else two_ref.at[k, 1, fields, :, my_q[1]]
                ),
                (line_send.at[3, k], line_recv.at[3 + part, k]),
            )

    def pack_states(k):
        for copy in load_states(k):
            copy.wait()

        def body(i, carry):
            window = pl.ds(pl.multiple_of(i * PIECE, PIECE), PIECE)
            for a in range(3):
                for h in range(2):
                    packed[k, i, a, h] = states[
                        k, a, window, pl.ds(h * LANES, LANES)
                    ].astype(jnp.bfloat16)
            return carry

        lax.fori_loop(0, PEERS, body, 0)

    def pack_grads(k):
        load_grads(k).wait()
        swap(k).wait_recv()
        low = slot_ref[2 * me] >= 0

        def body(i, carry):
            window = pl.ds(pl.multiple_of(i * PIECE, PIECE), PIECE)
            x = i // SIDE
            z = i % SIDE
            for h in range(2):
                columns = pl.ds(h * LANES, LANES)
                zero, one = (
                    grad_own[k, n, window, columns].astype(jnp.float32)
                    + grad_other[k, n, window, columns].astype(jnp.float32)
                    for n in range(2)
                )
                packed[k, i, 3, h] = jnp.where(low, zero, one).astype(jnp.bfloat16)
                if h == 0:
                    grad_line[k, h, x, z] = one.astype(jnp.bfloat16)
                else:
                    grad_line[k, h, z, x] = one.astype(jnp.bfloat16)
            return carry

        lax.fori_loop(0, PEERS, body, 0)

    def scatter_chunk(k):
        pack_states(k)
        pack_grads(k)
        scatter_second(k)
        scatter(k, 0, SPREAD)

    def step(k, n, h):
        source = landed[k]
        state = entry_t[0, n]
        first = entry_t[1 + h, n]
        last = entry_t[3 + h, n]
        twice = entry_t[5, n].astype(jnp.float32)
        scale = 1.0 / jnp.full((PIECE, LANES), entry_t[6, n].astype(jnp.float32))
        gradient = (
            source[first, h].astype(jnp.float32) + twice * source[last, h].astype(jnp.float32)
        ) * scale
        master = source[state, h].astype(jnp.float32)
        moment = source[state + 1, h].astype(jnp.float32)
        second = source[state + 2, h].astype(jnp.float32)
        moment = beta_one * moment + (1.0 - beta_one) * gradient
        second = beta_two * second + (1.0 - beta_two) * gradient * gradient
        master = master - learn_rate * (
            moment / (jnp.sqrt(second) + adam_eps) + decay_rate * master
        )
        return (
            master.astype(jnp.bfloat16), moment.astype(jnp.bfloat16), second.astype(jnp.bfloat16)
        )

    def update_second(k):
        def body(n, carry):
            for h in range(2):
                for a, value in enumerate(step(k, PEERS + h * SIDE * KEEP + n, h)):
                    update_two[k, h, n, a] = value
            return carry

        lax.fori_loop(0, SIDE * KEEP, body, 0)

    def update_first(k):
        def body(d, carry):
            for h in range(2):
                for a, value in enumerate(step(k, d, h)):
                    update_one[k, d, a, :, pl.ds(h * LANES, LANES)] = value
            return carry

        lax.fori_loop(0, PEERS, body, 0)

    def forward(k):
        window = pl.ds(k * rows, rows)
        pairs = (
            (one_ref.at[0, window], other_one_ref.at[window]),
            (two_ref.at[k, :, 0], other_two_ref.at[k]),
        )
        return [
            pltpu.make_async_remote_copy(
                src_ref=source,
                dst_ref=target,
                send_sem=fwd_send.at[k, n],
                recv_sem=fwd_recv.at[k, n],
                device_id=partner,
                device_id_type=MESH,
            )
            for n, (source, target) in enumerate(pairs)
        ]

    def all_bytes(ref, sem):
        pltpu.make_async_copy(ref, ref, sem).wait()

    def fill_both(d, carry):
        both_t[d] = jnp.where((slot_ref[2 * d] >= 0) & (slot_ref[2 * d + 1] >= 0), 1, 0)
        return carry

    def fill_rank(d, carry):
        place = (d // SIDE, d % SIDE)
        for h in range(2):
            p, q = place[1 - h], place[h]
            rank = jnp.int32(0)
            for j in range(SIDE - 1):
                rank = rank + jnp.where(j < q, both_t[line_device(h, p, j)], 0)
            rank_t[h, d] = jnp.minimum(rank, KEEP - 1)
        return carry

    def fill_grad(t, carry):
        d = t // 2
        place = (d // SIDE, d % SIDE)
        second = (t % 2 == 1) & (both_t[d] > 0)
        for h in range(2):
            kept = PEERS * SPREAD + KEEP * place[1 - h] + rank_t[h, d]
            grad_t[h, t] = jnp.where(second, kept, d * SPREAD + 3)
        return carry

    def fill_device(n, carry):
        p, r = n // KEEP, n % KEEP
        for h in range(2):
            found = jnp.int32(-1)
            for q in range(SIDE):
                d = line_device(h, p, q)
                found = jnp.where((both_t[d] > 0) & (rank_t[h, d] == r), d, found)
            device_t[h, n] = found
        return carry

    def fill_entry(n, slot):
        expert = jnp.maximum(slot_ref[slot], 0)
        holder = jnp.int32(0)
        for j in range(PEERS):
            holder = jnp.where(old_ref[j] == expert, j, holder)
        first = jnp.int32(0)
        last = jnp.int32(0)
        for t in range(2 * PEERS):
            last = jnp.where(slot_ref[t] == expert, t, last)
            back = 2 * PEERS - 1 - t
            first = jnp.where(slot_ref[back] == expert, back, first)
        entry_t[0, n] = holder * SPREAD
        for h in range(2):
            entry_t[1 + h, n] = grad_t[h, first]
            entry_t[3 + h, n] = grad_t[h, last]
        entry_t[5, n] = jnp.where(first == last, 0, 1)
        entry_t[6, n] = count_ref[expert]

    def fill_first(d, carry):
        fill_entry(d, 2 * d + jnp.where(slot_ref[2 * d] >= 0, 0, 1))
        return carry

    def fill_second(n, carry):
        for h in range(2):
            device = device_t[h, n]
            fill_entry(
                PEERS + h * SIDE * KEEP + n, jnp.where(device >= 0, 2 * device + 1, 0)
            )
        return carry

    for copy in tables:
        copy.start()
    for k in range(chunks):
        for copy in load_states(k) + [load_grads(k)]:
            copy.start()

    barrier = pltpu.get_barrier_semaphore()
    for other in targets:
        pl.semaphore_signal(
            barrier, inc=1, device_id=(core, other, plane), device_id_type=MESH
        )
    pl.semaphore_signal(barrier, inc=1, device_id=partner, device_id_type=MESH)
    for copy in tables:
        copy.wait()
    pack_states(0)
    pl.semaphore_wait(barrier, PEERS)

    for k in range(chunks):
        swap(k).start()

    scatter(0, 0, 3)
    lax.fori_loop(0, PEERS, fill_both, 0)
    lax.fori_loop(0, PEERS, fill_rank, 0)
    pack_grads(0)
    scatter_second(0)
    scatter(0, 3, 1)
    scatter_chunk(1)
    lax.fori_loop(0, 2 * PEERS, fill_grad, 0)
    lax.fori_loop(0, SIDE * KEEP, fill_device, 0)
    keep_grads(0)
    for k in range(2, AHEAD):
        scatter_chunk(k)
    lax.fori_loop(0, PEERS, fill_first, 0)
    lax.fori_loop(0, SIDE * KEEP, fill_second, 0)
    for h in range(2):
        slot = 2 * me + h
        held = jnp.where(slot_ref[slot] >= 0, 1, 0)
        owner = owner_ref[jnp.maximum(slot_ref[slot], 0)]
        flag_ref[pl.ds(h, 1)] = jnp.full((1, LANES), jnp.where(owner == slot, held, 0))
        flag_ref[pl.ds(2 + h, 1)] = jnp.full((1, LANES), held)
    flag_ref[pl.ds(4, 1)] = jnp.full((1, LANES), both_t[me])
    final = chunks - 1
    for k in range(chunks):
        if k + 1 < chunks:
            keep_grads(k + 1)
        all_bytes(landed[k].at[pl.ds(0, PEERS * SPREAD)], spread_recv.at[k])
        all_bytes(landed[k].at[pl.ds(PEERS * SPREAD, SIDE * KEEP)], line_recv.at[1, k])
        update_second(k)
        deliver_two(k)
        update_first(k)
        deliver_one(k)
        if k + AHEAD < chunks:
            scatter_chunk(k + AHEAD)
        if k > 0:
            pass_two(k - 1)
    pass_two(final)
    for k in range(chunks):
        one, two = forward(k)
        window = pl.ds(k * rows, rows)
        fields = pl.ds(*fields_of(k)[0])
        all_bytes(one_ref.at[fields, window], one_recv.at[k, 0])
        one.start()
        all_bytes(two_ref.at[k, :, fields], line_recv.at[3, k])
        two.start()
    rest = pl.ds(1, 2)
    all_bytes(one_ref.at[rest, pl.ds(final * rows, rows)], one_recv.at[final, 1])
    all_bytes(two_ref.at[final, :, rest], line_recv.at[4, final])
    for k in range(chunks):
        swap(k).wait_send()
        all_bytes(packed.at[k, pl.ds(0, PEERS - 1)], spread_send.at[k])
        all_bytes(update_one.at[k, pl.ds(0, PEERS - 1)], one_send.at[k])
        all_bytes(grad_line.at[k, :, pl.ds(0, SIDE - 1)], line_send.at[0, k])
        all_bytes(grad_kept.at[k, :, pl.ds(0, SIDE - 1)], line_send.at[1, k])
        all_bytes(update_two.at[k, :, pl.ds(0, KEEP * (SIDE - 1))], line_send.at[2, k])
        all_bytes(two_line.at[k, :, pl.ds(0, SIDE - 1)], line_send.at[3, k])
    for k in range(chunks):
        for copy in forward(k):
            copy.wait()


def short_expand_kernel(
    one_ref, two_ref, other_one_ref, other_two_ref, flag_ref,
    master_ref, moment_ref, second_ref, weight_ref,
    wide, narrow, sems, weight_sems,
):
    core = lax.axis_index("dp")
    half = one_ref.shape[1]
    steps, rows = wide.shape[1], wide.shape[3]
    outs = (master_ref, moment_ref, second_ref)

    def store(a, k):
        return pltpu.make_async_copy(
            wide.at[a, k], outs[a].at[:, pl.ds(k * rows, rows)], sems.at[a, k]
        )

    def weights(n, k):
        side = core if n == 0 else 1 - core
        return pltpu.make_async_copy(
            narrow.at[n, k],
            weight_ref.at[:, pl.ds(side * half + k * rows, rows)],
            weight_sems.at[n, k],
        )

    owned, held = ([flag_ref[pl.ds(n + h, 1)] > 0 for h in range(2)] for n in (0, 2))
    both = flag_ref[pl.ds(4, 1)] > 0
    for k in range(steps):
        window = pl.ds(k * rows, rows)
        for a in range(3):
            for h in range(2):
                columns = pl.ds(h * LANES, LANES)
                one = one_ref[a, window, columns].astype(jnp.float32)
                two = two_ref[k, h, a].reshape(rows, LANES).astype(jnp.float32)
                pick = jnp.where(both, two, one)
                wide[a, k, 0, :, columns] = jnp.where(owned[0], one, 0.0)
                wide[a, k, 1, :, columns] = jnp.where(owned[1], pick, 0.0)
                if a == 0:
                    narrow[0, k, 0, :, columns] = jnp.where(held[0], one, 0.0).astype(jnp.bfloat16)
                    narrow[0, k, 1, :, columns] = jnp.where(held[1], pick, 0.0).astype(jnp.bfloat16)
            store(a, k).start()
            if a == 0:
                weights(0, k).start()
        for h in range(2):
            columns = pl.ds(h * LANES, LANES)
            one = other_one_ref[window, columns].astype(jnp.float32)
            two = other_two_ref[k, h].reshape(rows, LANES).astype(jnp.float32)
            pick = jnp.where(both, two, one)
            narrow[1, k, 0, :, columns] = jnp.where(held[0], one, 0.0).astype(jnp.bfloat16)
            narrow[1, k, 1, :, columns] = jnp.where(held[1], pick, 0.0).astype(jnp.bfloat16)
        weights(1, k).start()
    for k in range(steps):
        for a in range(3):
            store(a, k).wait()
        for n in range(2):
            weights(n, k).wait()


def short_kernel_allowed(slot_hbm, ok_ref, slot_ref, sem):
    copy = pltpu.make_async_copy(slot_hbm, slot_ref, sem)
    copy.start()
    copy.wait()
    both = [
        jnp.where((slot_ref[2 * d] >= 0) & (slot_ref[2 * d + 1] >= 0), 1, 0) for d in range(PEERS)
    ]
    most = jnp.int32(0)
    for h in range(2):
        for p in range(SIDE):
            line = [both[line_device(h, p, q)] for q in range(SIDE)]
            most = jnp.maximum(most, line[0] + line[1] + line[2] + line[3])
    ok_ref[0] = jnp.where(most <= KEEP, 1, 0)


def in_hbm(*arrays):
    return [pltpu.with_memory_space_constraint(a, pltpu.HBM) for a in arrays]


def short_exchange(
    master_old, moment_old, second_old, grad_parts, old_expert, slot_expert, owner_slot, token_count
):
    half, width = master_old.shape[1:]
    rows = PEERS * PIECE
    chunks = half // rows
    anywhere = pl.BlockSpec(memory_space=pl.ANY)
    vmem = pl.BlockSpec(memory_space=pltpu.VMEM)
    bf16 = jnp.bfloat16
    dma = pltpu.SemaphoreType.DMA
    piece = (PIECE, LANES)
    smem = lambda *shape: pltpu.SMEM(shape, jnp.int32)
    delivered = pl.pallas_call(
        functools.partial(short_kernel, chunks),
        out_shape=(
            pltpu.VMEM((3, half, width), bf16),
            pltpu.VMEM((chunks, 2, 3, SIDE, SIDE, *piece), bf16),
            pltpu.VMEM((half, width), bf16),
            pltpu.VMEM((chunks, 2, SIDE, SIDE, *piece), bf16),
            pltpu.VMEM((8, LANES), jnp.int32),
        ),
        in_specs=[anywhere] * 8,
        out_specs=(vmem,) * 5,
        scratch_shapes=[pltpu.VMEM((PEERS * SPREAD + SIDE * KEEP, 2, *piece), bf16)] * chunks
        + [pltpu.VMEM((2, SIDE, SIDE, *piece), bf16)] * chunks
        + [pltpu.VMEM((2, SIDE, KEEP, 3, *piece), bf16)] * chunks
        + [
            pltpu.VMEM((chunks, 3, rows, width), jnp.float32),
            pltpu.VMEM((chunks, 2, rows, width), bf16),
            pltpu.VMEM((chunks, 2, rows, width), bf16),
            pltpu.VMEM((chunks, PEERS, SPREAD, 2, *piece), bf16),
            pltpu.VMEM((chunks, 2, SIDE, SIDE, *piece), bf16),
            pltpu.VMEM((chunks, 2, SIDE, KEEP, *piece), bf16),
            pltpu.VMEM((chunks, PEERS, 3, PIECE, width), bf16),
            pltpu.VMEM((chunks, 2, SIDE * KEEP, 3, *piece), bf16),
            pltpu.VMEM((chunks, 2, SIDE, 3, SIDE, *piece), bf16),
            smem(PEERS),
            smem(2 * PEERS),
            smem(PEERS),
            smem(PEERS),
            smem(PEERS),
            smem(2, PEERS),
            smem(2, 2 * PEERS),
            smem(2, SIDE * KEEP),
            smem(7, 2 * PEERS),
            dma((4,)),
            dma((chunks, 4)),
            dma((chunks,)),
            dma((chunks,)),
            dma((chunks,)),
            dma((chunks,)),
            dma((4, chunks)),
            dma((5, chunks)),
            dma((chunks,)),
            dma((chunks, 2)),
            dma((chunks, 2)),
            dma((chunks, 2)),
        ],
        compiler_params=pltpu.CompilerParams(
            collective_id=1, has_side_effects=True, vmem_limit_bytes=40 << 20
        ),
        name="short_exchange",
    )(
        *in_hbm(
            old_expert, slot_expert, owner_slot, token_count,
            master_old, moment_old, second_old, grad_parts,
        )
    )
    wide = jax.ShapeDtypeStruct((2, half, width), jnp.float32)
    return pl.pallas_call(
        short_expand_kernel,
        out_shape=(wide, wide, wide, jax.ShapeDtypeStruct((2, 2 * half, width), bf16)),
        in_specs=[vmem] * 5,
        out_specs=(anywhere,) * 4,
        scratch_shapes=[
            pltpu.VMEM((3, chunks, 2, rows, width), jnp.float32),
            pltpu.VMEM((2, chunks, 2, rows, width), bf16),
            dma((3, chunks)),
            dma((2, chunks)),
        ],
        compiler_params=pltpu.CompilerParams(vmem_limit_bytes=24 << 20),
        name="short_expand",
    )(*delivered)


def per_device(*args):
    slot_expert = args[5]
    allowed = pl.pallas_call(
        short_kernel_allowed,
        out_shape=jax.ShapeDtypeStruct((1,), jnp.int32),
        in_specs=[pl.BlockSpec(memory_space=pl.ANY)],
        out_specs=pl.BlockSpec(memory_space=pltpu.SMEM),
        scratch_shapes=[pltpu.SMEM(slot_expert.shape, jnp.int32), pltpu.SemaphoreType.DMA],
        name="allowed",
    )(*in_hbm(slot_expert))
    return lax.cond(allowed[0] > 0, short_exchange, full_exchange, *args)


def solution(mesh):
    placed = (
        P("expert", "dp", "etp"),
        P("expert", "dp", "etp"),
        P("expert", "dp", "etp"),
        P("dp", "expert", None, "etp"),
        P(),
        P(),
        P(),
        P(),
    )
    return jax.shard_map(
        per_device,
        mesh=mesh,
        in_specs=placed,
        out_specs=(
            P("expert", "dp", "etp"),
            P("expert", "dp", "etp"),
            P("expert", "dp", "etp"),
            P("expert", None, "etp"),
        ),
        check_vma=False,
    )
```

```python
import functools

import jax
import jax.numpy as jnp
from jax import lax
from jax.experimental import pallas as pl
from jax.experimental.pallas import tpu as pltpu
from jax.sharding import PartitionSpec as P

beta_one = 0.9
beta_two = 0.95
learn_rate = 0.05
decay_rate = 0.1
adam_eps = 1e-08

MESH = pl.DeviceIdType.MESH
SIDE = 4
PEERS = SIDE * SIDE
FIELDS = 5
RESULTS = 6
PIECE = 16
ORDER = (
    (0, 1), (0, 3), (1, 0), (3, 0), (1, 1), (3, 3), (1, 3), (3, 1),
    (0, 2), (2, 0), (2, 1), (2, 3), (1, 2), (3, 2), (2, 2),
)


def exchange_kernel(
    chunks,
    old_hbm, slot_hbm, owner_hbm, count_hbm,
    master_ref, moment_ref, second_ref, grad_ref,
    out_ref, other_ref,
    *scratch,
):
    landed = scratch[:chunks]
    (states, grad_own, grad_other, packed, updated, table,
     old_ref, slot_ref, owner_ref, count_ref, table_sem,
     load_sem, dp_send, dp_recv, send_one, recv_one, send_two, recv_two,
     fwd_send, fwd_recv) = scratch[chunks:]
    tables = [
        pltpu.make_async_copy(source, held, table_sem.at[n])
        for n, (source, held) in enumerate(
            ((old_hbm, old_ref), (slot_hbm, slot_ref), (owner_hbm, owner_ref), (count_hbm, count_ref))
        )
    ]
    rows = states.shape[2]
    half = chunks * rows
    core = lax.axis_index("dp")
    me = lax.axis_index("expert")
    plane = lax.axis_index("etp")
    my_x = me // SIDE
    my_z = me % SIDE
    partner = (1 - core, me, plane)
    targets = [
        lax.rem(my_x + dx, SIDE) * SIDE + lax.rem(my_z + dz, SIDE) for dx, dz in ORDER
    ]

    def load_states(k):
        window = pl.ds(k * rows, rows)
        return [
            pltpu.make_async_copy(ref.at[0, window], states.at[k, a], load_sem.at[k, a])
            for a, ref in enumerate((master_ref, moment_ref, second_ref))
        ]

    def load_grads(k):
        return pltpu.make_async_copy(
            grad_ref.at[0, :, pl.ds(core * half + k * rows, rows)],
            grad_own.at[k],
            load_sem.at[k, 3],
        )

    def swap(k):
        return pltpu.make_async_remote_copy(
            src_ref=grad_ref.at[0, :, pl.ds((1 - core) * half + k * rows, rows)],
            dst_ref=grad_other.at[k],
            send_sem=dp_send.at[k],
            recv_sem=dp_recv.at[k],
            device_id=partner,
            device_id_type=MESH,
        )

    def spread(source, target, send, recv):
        for other in targets:
            pltpu.make_async_remote_copy(
                src_ref=source(other),
                dst_ref=target,
                send_sem=send,
                recv_sem=recv,
                device_id=(core, other, plane),
                device_id_type=MESH,
            ).start()
        pltpu.make_async_copy(source(me), target, recv).start()

    def scatter(k, first, count):
        spread(
            lambda i: packed.at[k, i, pl.ds(first, count)],
            landed[k].at[pl.ds(me * FIELDS + first, count)],
            send_one.at[k],
            recv_one.at[k],
        )

    def deliver(k, first, count, part):
        window = pl.ds(k * rows + me * PIECE, PIECE)
        spread(
            lambda i: updated.at[k, i, pl.ds(first, count)],
            out_ref.at[pl.ds(first, count), window],
            send_two.at[k],
            recv_two.at[k, part],
        )

    def pack_states(k):
        for copy in load_states(k):
            copy.wait()

        def body(i, carry):
            window = pl.ds(pl.multiple_of(i * PIECE, PIECE), PIECE)
            for a in range(3):
                packed[k, i, a] = states[k, a, window].astype(jnp.bfloat16)
            return carry

        lax.fori_loop(0, PEERS, body, 0)

    def pack_grads(k):
        load_grads(k).wait()
        swap(k).wait_recv()

        def body(i, carry):
            window = pl.ds(pl.multiple_of(i * PIECE, PIECE), PIECE)
            for h in range(2):
                packed[k, i, 3 + h] = (
                    grad_own[k, h, window].astype(jnp.float32)
                    + grad_other[k, h, window].astype(jnp.float32)
                ).astype(jnp.bfloat16)
            return carry

        lax.fori_loop(0, PEERS, body, 0)

    def update(k):
        source = landed[k]

        def body(d, carry):
            for h in range(2):
                s = 2 * d + h
                state = table[0, s]
                first = table[1, s]
                last = table[2, s]
                twice = table[3, s].astype(jnp.float32)
                scale = 1.0 / jnp.full((PIECE, 256), table[4, s].astype(jnp.float32))
                gradient = (
                    source[first].astype(jnp.float32)
                    + twice * source[last].astype(jnp.float32)
                ) * scale
                master = source[state].astype(jnp.float32)
                moment = source[state + 1].astype(jnp.float32)
                second = source[state + 2].astype(jnp.float32)
                moment = beta_one * moment + (1.0 - beta_one) * gradient
                second = beta_two * second + (1.0 - beta_two) * gradient * gradient
                master = master - learn_rate * (
                    moment / (jnp.sqrt(second) + adam_eps) + decay_rate * master
                )
                held = table[5, s] > 0
                owned = table[6, s] > 0
                updated[k, d, h] = jnp.where(held, master, 0.0).astype(jnp.bfloat16)
                updated[k, d, 2 + h] = jnp.where(owned, moment, 0.0).astype(jnp.bfloat16)
                updated[k, d, 4 + h] = jnp.where(owned, second, 0.0).astype(jnp.bfloat16)
            return carry

        lax.fori_loop(0, PEERS, body, 0)

    def forward(k):
        window = pl.ds(k * rows, rows)
        return pltpu.make_async_remote_copy(
            src_ref=out_ref.at[pl.ds(0, 2), window],
            dst_ref=other_ref.at[:, window],
            send_sem=fwd_send.at[k],
            recv_sem=fwd_recv.at[k],
            device_id=partner,
            device_id_type=MESH,
        )

    def all_bytes(ref, sem):
        pltpu.make_async_copy(ref, ref, sem).wait()

    for copy in tables:
        copy.start()
    for k in range(chunks):
        for copy in load_states(k) + [load_grads(k)]:
            copy.start()

    barrier = pltpu.get_barrier_semaphore()
    for other in targets:
        pl.semaphore_signal(
            barrier, inc=1, device_id=(core, other, plane), device_id_type=MESH
        )
    pl.semaphore_signal(barrier, inc=1, device_id=partner, device_id_type=MESH)
    pack_states(0)
    pl.semaphore_wait(barrier, PEERS)

    for k in range(chunks):
        swap(k).start()

    def fill_table(s, carry):
        expert = jnp.maximum(slot_ref[s], 0)
        holder = jnp.int32(0)
        for j in range(PEERS):
            holder = jnp.where(old_ref[j] == expert, j, holder)
        first = jnp.int32(0)
        last = jnp.int32(0)
        for t in range(2 * PEERS):
            last = jnp.where(slot_ref[t] == expert, t, last)
            back = 2 * PEERS - 1 - t
            first = jnp.where(slot_ref[back] == expert, back, first)
        table[0, s] = holder * FIELDS
        table[1, s] = (first // 2) * FIELDS + 3 + first % 2
        table[2, s] = (last // 2) * FIELDS + 3 + last % 2
        table[3, s] = jnp.where(first == last, 0, 1)
        table[4, s] = count_ref[expert]
        table[5, s] = jnp.where(slot_ref[s] >= 0, 1, 0)
        table[6, s] = jnp.where((slot_ref[s] >= 0) & (owner_ref[expert] == s), 1, 0)
        return carry

    scatter(0, 0, 3)
    pack_grads(0)
    scatter(0, 3, 2)
    pack_states(1)
    pack_grads(1)
    scatter(1, 0, FIELDS)
    for copy in tables:
        copy.wait()
    lax.fori_loop(0, 2 * PEERS, fill_table, 0)
    final = chunks - 1
    for k in range(chunks):
        all_bytes(landed[k], recv_one.at[k])
        update(k)
        if k < final:
            deliver(k, 0, RESULTS, 0)
        else:
            deliver(k, 0, 2, 0)
            deliver(k, 2, 4, 1)
        if k + 2 < chunks:
            pack_states(k + 2)
            pack_grads(k + 2)
            scatter(k + 2, 0, FIELDS)
    for k in range(chunks):
        fields = pl.ds(0, RESULTS if k < final else 2)
        all_bytes(out_ref.at[fields, pl.ds(k * rows, rows)], recv_two.at[k, 0])
        forward(k).start()
    all_bytes(out_ref.at[pl.ds(2, 4), pl.ds(final * rows, rows)], recv_two.at[final, 1])
    for k in range(chunks):
        swap(k).wait_send()
        all_bytes(packed.at[k, pl.ds(0, PEERS - 1)], send_one.at[k])
        all_bytes(updated.at[k, pl.ds(0, PEERS - 1)], send_two.at[k])
    for k in range(chunks):
        forward(k).wait()


def expand_kernel(
    slot_hbm, owner_hbm, here_ref, there_ref,
    master_ref, moment_ref, second_ref, weight_ref,
    wide, slot_ref, owner_ref, sems, weight_sems, table_sems,
):
    core = lax.axis_index("dp")
    me = lax.axis_index("expert")
    half = here_ref.shape[1]
    steps, rows = wide.shape[1], wide.shape[3]
    outs = (master_ref, moment_ref, second_ref)
    weights = [
        pltpu.make_async_copy(
            here_ref.at[pl.ds(0, 2)], weight_ref.at[:, pl.ds(core * half, half)], weight_sems.at[0]
        ),
        pltpu.make_async_copy(
            there_ref, weight_ref.at[:, pl.ds((1 - core) * half, half)], weight_sems.at[1]
        ),
    ]

    def store(a, k):
        return pltpu.make_async_copy(
            wide.at[a, k], outs[a].at[:, pl.ds(k * rows, rows)], sems.at[a, k]
        )

    tables = [
        pltpu.make_async_copy(slot_hbm, slot_ref, table_sems.at[0]),
        pltpu.make_async_copy(owner_hbm, owner_ref, table_sems.at[1]),
    ]
    for copy in tables + weights:
        copy.start()
    for a in (1, 2):
        for k in range(steps):
            for h in range(2):
                wide[a, k, h] = here_ref[2 * a + h, pl.ds(k * rows, rows)].astype(jnp.float32)
            store(a, k).start()
    for copy in tables:
        copy.wait()
    owned = []
    for h in range(2):
        slot = 2 * me + h
        expert = slot_ref[slot]
        owned.append((expert >= 0) & (owner_ref[jnp.maximum(expert, 0)] == slot))
    for k in range(steps):
        for h in range(2):
            value = here_ref[h, pl.ds(k * rows, rows)].astype(jnp.float32)
            wide[0, k, h] = jnp.where(owned[h], value, 0.0)
        store(0, k).start()
    for copy in weights:
        copy.wait()
    for k in range(steps):
        for a in range(3):
            store(a, k).wait()


def full_exchange(
    master_old, moment_old, second_old, grad_parts, old_expert, slot_expert, owner_slot, token_count
):
    half, width = master_old.shape[1:]
    rows = PEERS * PIECE
    chunks = half // rows
    anywhere = pl.BlockSpec(memory_space=pl.ANY)
    vmem = pl.BlockSpec(memory_space=pltpu.VMEM)
    bf16 = jnp.bfloat16
    dma = pltpu.SemaphoreType.DMA
    here, there = pl.pallas_call(
        functools.partial(exchange_kernel, chunks),
        out_shape=(
            pltpu.VMEM((RESULTS, half, width), bf16),
            pltpu.VMEM((2, half, width), bf16),
        ),
        in_specs=[anywhere] * 8,
        out_specs=(vmem, vmem),
        scratch_shapes=[pltpu.VMEM((PEERS * FIELDS, PIECE, width), bf16)] * chunks
        + [
            pltpu.VMEM((chunks, 3, rows, width), jnp.float32),
            pltpu.VMEM((chunks, 2, rows, width), bf16),
            pltpu.VMEM((chunks, 2, rows, width), bf16),
            pltpu.VMEM((chunks, PEERS, FIELDS, PIECE, width), bf16),
            pltpu.VMEM((chunks, PEERS, RESULTS, PIECE, width), bf16),
            pltpu.SMEM((7, 2 * PEERS), jnp.int32),
            pltpu.SMEM(old_expert.shape, jnp.int32),
            pltpu.SMEM(slot_expert.shape, jnp.int32),
            pltpu.SMEM(owner_slot.shape, jnp.int32),
            pltpu.SMEM(token_count.shape, jnp.int32),
            dma((4,)),
            dma((chunks, 4)),
            dma((chunks,)),
            dma((chunks,)),
            dma((chunks,)),
            dma((chunks,)),
            dma((chunks,)),
            dma((chunks, 2)),
            dma((chunks,)),
            dma((chunks,)),
        ],
        compiler_params=pltpu.CompilerParams(
            collective_id=0, has_side_effects=True, vmem_limit_bytes=40 << 20
        ),
        name="exchange",
    )(
        *(
            pltpu.with_memory_space_constraint(a, pltpu.HBM)
            for a in (
                old_expert, slot_expert, owner_slot, token_count,
                master_old, moment_old, second_old, grad_parts,
            )
        ),
    )

    steps = 7
    wide = jax.ShapeDtypeStruct((2, half, width), jnp.float32)
    return pl.pallas_call(
        expand_kernel,
        out_shape=(wide, wide, wide, jax.ShapeDtypeStruct((2, 2 * half, width), bf16)),
        in_specs=[anywhere, anywhere, vmem, vmem],
        out_specs=(anywhere,) * 4,
        scratch_shapes=[
            pltpu.VMEM((3, steps, 2, half // steps, width), jnp.float32),
            pltpu.SMEM(slot_expert.shape, jnp.int32),
            pltpu.SMEM(owner_slot.shape, jnp.int32),
            dma((3, steps)),
            dma((2,)),
            dma((2,)),
        ],
        compiler_params=pltpu.CompilerParams(vmem_limit_bytes=24 << 20),
        name="expand",
    )(
        pltpu.with_memory_space_constraint(slot_expert, pltpu.HBM),
        pltpu.with_memory_space_constraint(owner_slot, pltpu.HBM),
        here,
        there,
    )


LANES = 128
AHEAD = 4
SPREAD = 4


def line_device(h, p, q):
    return q * SIDE + p if h == 0 else p * SIDE + q


def short_kernel(
    chunks, keep,
    old_hbm, slot_hbm, owner_hbm, count_hbm,
    master_ref, moment_ref, second_ref, grad_ref,
    one_ref, two_ref, other_one_ref, other_two_ref, flag_ref,
    *scratch,
):
    landed = scratch[:chunks]
    relay_grad = scratch[chunks : 2 * chunks]
    relay_two = scratch[2 * chunks : 3 * chunks]
    (states, grad_own, grad_other, packed, grad_line, grad_kept,
     update_one, update_two, two_line,
     old_ref, slot_ref, owner_ref, count_ref, both_t, rank_t, grad_t, device_t, entry_t, table_sem,
     load_sem, dp_send, dp_recv, spread_send, spread_recv, line_send, line_recv,
     one_send, one_recv, fwd_send, fwd_recv) = scratch[3 * chunks :]
    rows = states.shape[2]
    half = chunks * rows
    core = lax.axis_index("dp")
    me = lax.axis_index("expert")
    plane = lax.axis_index("etp")
    my_x = me // SIDE
    my_z = me % SIDE
    my_p = (my_z, my_x)
    my_q = (my_x, my_z)
    partner = (1 - core, me, plane)
    targets = [
        lax.rem(my_x + dx, SIDE) * SIDE + lax.rem(my_z + dz, SIDE) for dx, dz in ORDER
    ]
    tables = [
        pltpu.make_async_copy(source, held, table_sem.at[n])
        for n, (source, held) in enumerate(
            ((old_hbm, old_ref), (slot_hbm, slot_ref), (owner_hbm, owner_ref), (count_hbm, count_ref))
        )
    ]

    def load_states(k):
        window = pl.ds(k * rows, rows)
        return [
            pltpu.make_async_copy(ref.at[0, window], states.at[k, a], load_sem.at[k, a])
            for a, ref in enumerate((master_ref, moment_ref, second_ref))
        ]

    def load_grads(k):
        return pltpu.make_async_copy(
            grad_ref.at[0, :, pl.ds(core * half + k * rows, rows)],
            grad_own.at[k],
            load_sem.at[k, 3],
        )

    def swap(k):
        return pltpu.make_async_remote_copy(
            src_ref=grad_ref.at[0, :, pl.ds((1 - core) * half + k * rows, rows)],
            dst_ref=grad_other.at[k],
            send_sem=dp_send.at[k],
            recv_sem=dp_recv.at[k],
            device_id=partner,
            device_id_type=MESH,
        )

    def send(source, target, sems, other):
        pltpu.make_async_remote_copy(
            src_ref=source,
            dst_ref=target,
            send_sem=sems[0],
            recv_sem=sems[1],
            device_id=(core, other, plane),
            device_id_type=MESH,
        ).start()

    def spread(source, target, sems):
        for other in targets:
            send(source(other), target, sems, other)
        pltpu.make_async_copy(source(me), target, sems[1]).start()

    def along_line(use_p, source, target, sems):
        for step in (1, 3, 2):
            for h in range(2):
                if use_p:
                    place = lax.rem(my_p[h] + step, SIDE)
                    other = line_device(h, place, my_q[h])
                else:
                    place = lax.rem(my_q[h] + step, SIDE)
                    other = line_device(h, my_p[h], place)
                send(source(h, place), target(h), sems, other)
        for h in range(2):
            place = my_p[h] if use_p else my_q[h]
            pltpu.make_async_copy(source(h, place), target(h), sems[1]).start()

    def scatter(k, first, count):
        spread(
            lambda i: packed.at[k, i, pl.ds(first, count)],
            landed[k].at[pl.ds(me * SPREAD + first, count)],
            (spread_send.at[k], spread_recv.at[k]),
        )

    def scatter_second(k):
        along_line(
            False,
            lambda h, q: grad_line.at[k, h, q],
            lambda h: relay_grad[k].at[h, my_q[h]],
            (line_send.at[0, k], line_recv.at[0, k]),
        )

    def keep_grads(k):
        all_bytes(relay_grad[k], line_recv.at[0, k])
        for h in range(2):
            for r in range(keep):
                device = jnp.maximum(device_t[h, keep * my_p[h] + r], 0)
                q = device // SIDE if h == 0 else device % SIDE
                for p in range(SIDE):
                    grad_kept[k, h, p, r] = relay_grad[k][h, q, p]
        along_line(
            True,
            lambda h, p: grad_kept.at[k, h, p],
            lambda h: landed[k].at[pl.ds(PEERS * SPREAD + keep * my_p[h], keep), h],
            (line_send.at[1, k], line_recv.at[1, k]),
        )

    def fields_of(k):
        return ((0, 3),) if k < chunks - 1 else ((0, 1), (1, 2))

    def deliver_one(k):
        for part, (first, count) in enumerate(fields_of(k)):
            fields = pl.ds(first, count)
            spread(
                lambda i: update_one.at[k, i, fields],
                one_ref.at[fields, pl.ds(k * rows + me * PIECE, PIECE)],
                (one_send.at[k], one_recv.at[k, part]),
            )

    def deliver_two(k):
        along_line(
            True,
            lambda h, p: update_two.at[k, h, pl.ds(keep * p, keep)],
            lambda h: relay_two[k].at[h, my_p[h]],
            (line_send.at[2, k], line_recv.at[2, k]),
        )

    def pass_two(k):
        all_bytes(relay_two[k], line_recv.at[2, k])

        def body(q, carry):
            for h in range(2):
                r = rank_t[h, line_device(h, my_p[h], q)]
                for a in range(3):
                    for p in range(SIDE):
                        two_line[k, h, q, a, p] = relay_two[k][h, p, r, a]
            return carry

        lax.fori_loop(0, SIDE, body, 0)
        for part, (first, count) in enumerate(fields_of(k)):
            fields = pl.ds(first, count)
            along_line(
                False,
                lambda h, q: two_line.at[k, h, q, fields],
                lambda h: (
                    two_ref.at[k, 0, fields, my_q[0]]
                    if h == 0
                    else two_ref.at[k, 1, fields, :, my_q[1]]
                ),
                (line_send.at[3, k], line_recv.at[3 + part, k]),
            )

    def pack_states(k):
        for copy in load_states(k):
            copy.wait()

        def body(i, carry):
            window = pl.ds(pl.multiple_of(i * PIECE, PIECE), PIECE)
            for a in range(3):
                for h in range(2):
                    packed[k, i, a, h] = states[
                        k, a, window, pl.ds(h * LANES, LANES)
                    ].astype(jnp.bfloat16)
            return carry

        lax.fori_loop(0, PEERS, body, 0)

    def pack_grads(k):
        load_grads(k).wait()
        swap(k).wait_recv()
        low = slot_ref[2 * me] >= 0

        def body(i, carry):
            window = pl.ds(pl.multiple_of(i * PIECE, PIECE), PIECE)
            x = i // SIDE
            z = i % SIDE
            for h in range(2):
                columns = pl.ds(h * LANES, LANES)
                zero, one = (
                    grad_own[k, n, window, columns].astype(jnp.float32)
                    + grad_other[k, n, window, columns].astype(jnp.float32)
                    for n in range(2)
                )
                packed[k, i, 3, h] = jnp.where(low, zero, one).astype(jnp.bfloat16)
                if h == 0:
                    grad_line[k, h, x, z] = one.astype(jnp.bfloat16)
                else:
                    grad_line[k, h, z, x] = one.astype(jnp.bfloat16)
            return carry

        lax.fori_loop(0, PEERS, body, 0)

    def scatter_chunk(k):
        pack_states(k)
        pack_grads(k)
        scatter_second(k)
        scatter(k, 0, SPREAD)

    def step(k, n, h):
        source = landed[k]
        state = entry_t[0, n]
        first = entry_t[1 + h, n]
        last = entry_t[3 + h, n]
        twice = entry_t[5, n].astype(jnp.float32)
        scale = 1.0 / jnp.full((PIECE, LANES), entry_t[6, n].astype(jnp.float32))
        gradient = (
            source[first, h].astype(jnp.float32) + twice * source[last, h].astype(jnp.float32)
        ) * scale
        master = source[state, h].astype(jnp.float32)
        moment = source[state + 1, h].astype(jnp.float32)
        second = source[state + 2, h].astype(jnp.float32)
        moment = beta_one * moment + (1.0 - beta_one) * gradient
        second = beta_two * second + (1.0 - beta_two) * gradient * gradient
        master = master - learn_rate * (
            moment / (jnp.sqrt(second) + adam_eps) + decay_rate * master
        )
        return (
            master.astype(jnp.bfloat16), moment.astype(jnp.bfloat16), second.astype(jnp.bfloat16)
        )

    def update_second(k):
        def body(n, carry):
            for h in range(2):
                for a, value in enumerate(step(k, PEERS + h * SIDE * keep + n, h)):
                    update_two[k, h, n, a] = value
            return carry

        lax.fori_loop(0, SIDE * keep, body, 0)

    def update_first(k):
        def body(d, carry):
            for h in range(2):
                for a, value in enumerate(step(k, d, h)):
                    update_one[k, d, a, :, pl.ds(h * LANES, LANES)] = value
            return carry

        lax.fori_loop(0, PEERS, body, 0)

    def forward(k):
        window = pl.ds(k * rows, rows)
        pairs = (
            (one_ref.at[0, window], other_one_ref.at[window]),
            (two_ref.at[k, :, 0], other_two_ref.at[k]),
        )
        return [
            pltpu.make_async_remote_copy(
                src_ref=source,
                dst_ref=target,
                send_sem=fwd_send.at[k, n],
                recv_sem=fwd_recv.at[k, n],
                device_id=partner,
                device_id_type=MESH,
            )
            for n, (source, target) in enumerate(pairs)
        ]

    def all_bytes(ref, sem):
        pltpu.make_async_copy(ref, ref, sem).wait()

    def fill_both(d, carry):
        both_t[d] = jnp.where((slot_ref[2 * d] >= 0) & (slot_ref[2 * d + 1] >= 0), 1, 0)
        return carry

    def fill_rank(d, carry):
        place = (d // SIDE, d % SIDE)
        for h in range(2):
            p, q = place[1 - h], place[h]
            rank = jnp.int32(0)
            for j in range(SIDE - 1):
                rank = rank + jnp.where(j < q, both_t[line_device(h, p, j)], 0)
            rank_t[h, d] = jnp.minimum(rank, keep - 1)
        return carry

    def fill_grad(t, carry):
        d = t // 2
        place = (d // SIDE, d % SIDE)
        second = (t % 2 == 1) & (both_t[d] > 0)
        for h in range(2):
            kept = PEERS * SPREAD + keep * place[1 - h] + rank_t[h, d]
            grad_t[h, t] = jnp.where(second, kept, d * SPREAD + 3)
        return carry

    def fill_device(n, carry):
        p, r = n // keep, n % keep
        for h in range(2):
            found = jnp.int32(-1)
            for q in range(SIDE):
                d = line_device(h, p, q)
                found = jnp.where((both_t[d] > 0) & (rank_t[h, d] == r), d, found)
            device_t[h, n] = found
        return carry

    def fill_entry(n, slot):
        expert = jnp.maximum(slot_ref[slot], 0)
        holder = jnp.int32(0)
        for j in range(PEERS):
            holder = jnp.where(old_ref[j] == expert, j, holder)
        first = jnp.int32(0)
        last = jnp.int32(0)
        for t in range(2 * PEERS):
            last = jnp.where(slot_ref[t] == expert, t, last)
            back = 2 * PEERS - 1 - t
            first = jnp.where(slot_ref[back] == expert, back, first)
        entry_t[0, n] = holder * SPREAD
        for h in range(2):
            entry_t[1 + h, n] = grad_t[h, first]
            entry_t[3 + h, n] = grad_t[h, last]
        entry_t[5, n] = jnp.where(first == last, 0, 1)
        entry_t[6, n] = count_ref[expert]

    def fill_first(d, carry):
        fill_entry(d, 2 * d + jnp.where(slot_ref[2 * d] >= 0, 0, 1))
        return carry

    def fill_second(n, carry):
        for h in range(2):
            device = device_t[h, n]
            fill_entry(
                PEERS + h * SIDE * keep + n, jnp.where(device >= 0, 2 * device + 1, 0)
            )
        return carry

    for copy in tables:
        copy.start()
    for k in range(chunks):
        for copy in load_states(k) + [load_grads(k)]:
            copy.start()

    barrier = pltpu.get_barrier_semaphore()
    for other in targets:
        pl.semaphore_signal(
            barrier, inc=1, device_id=(core, other, plane), device_id_type=MESH
        )
    pl.semaphore_signal(barrier, inc=1, device_id=partner, device_id_type=MESH)
    for copy in tables:
        copy.wait()
    pack_states(0)
    pl.semaphore_wait(barrier, PEERS)

    for k in range(chunks):
        swap(k).start()

    scatter(0, 0, 3)
    lax.fori_loop(0, PEERS, fill_both, 0)
    lax.fori_loop(0, PEERS, fill_rank, 0)
    pack_grads(0)
    scatter_second(0)
    scatter(0, 3, 1)
    scatter_chunk(1)
    lax.fori_loop(0, 2 * PEERS, fill_grad, 0)
    lax.fori_loop(0, SIDE * keep, fill_device, 0)
    keep_grads(0)
    for k in range(2, AHEAD):
        scatter_chunk(k)
    lax.fori_loop(0, PEERS, fill_first, 0)
    lax.fori_loop(0, SIDE * keep, fill_second, 0)
    for h in range(2):
        slot = 2 * me + h
        held = jnp.where(slot_ref[slot] >= 0, 1, 0)
        owner = owner_ref[jnp.maximum(slot_ref[slot], 0)]
        flag_ref[pl.ds(h, 1)] = jnp.full((1, LANES), jnp.where(owner == slot, held, 0))
        flag_ref[pl.ds(2 + h, 1)] = jnp.full((1, LANES), held)
    flag_ref[pl.ds(4, 1)] = jnp.full((1, LANES), both_t[me])
    final = chunks - 1
    for k in range(chunks):
        if k + 1 < chunks:
            keep_grads(k + 1)
        all_bytes(landed[k].at[pl.ds(0, PEERS * SPREAD)], spread_recv.at[k])
        all_bytes(landed[k].at[pl.ds(PEERS * SPREAD, SIDE * keep)], line_recv.at[1, k])
        update_second(k)
        deliver_two(k)
        update_first(k)
        deliver_one(k)
        if k + AHEAD < chunks:
            scatter_chunk(k + AHEAD)
        if k > 0:
            pass_two(k - 1)
    pass_two(final)
    for k in range(chunks):
        one, two = forward(k)
        window = pl.ds(k * rows, rows)
        fields = pl.ds(*fields_of(k)[0])
        all_bytes(one_ref.at[fields, window], one_recv.at[k, 0])
        one.start()
        all_bytes(two_ref.at[k, :, fields], line_recv.at[3, k])
        two.start()
    rest = pl.ds(1, 2)
    all_bytes(one_ref.at[rest, pl.ds(final * rows, rows)], one_recv.at[final, 1])
    all_bytes(two_ref.at[final, :, rest], line_recv.at[4, final])
    for k in range(chunks):
        swap(k).wait_send()
        all_bytes(packed.at[k, pl.ds(0, PEERS - 1)], spread_send.at[k])
        all_bytes(update_one.at[k, pl.ds(0, PEERS - 1)], one_send.at[k])
        all_bytes(grad_line.at[k, :, pl.ds(0, SIDE - 1)], line_send.at[0, k])
        all_bytes(grad_kept.at[k, :, pl.ds(0, SIDE - 1)], line_send.at[1, k])
        all_bytes(update_two.at[k, :, pl.ds(0, keep * (SIDE - 1))], line_send.at[2, k])
        all_bytes(two_line.at[k, :, pl.ds(0, SIDE - 1)], line_send.at[3, k])
    for k in range(chunks):
        for copy in forward(k):
            copy.wait()


def short_expand_kernel(
    one_ref, two_ref, other_one_ref, other_two_ref, flag_ref,
    master_ref, moment_ref, second_ref, weight_ref,
    wide, narrow, sems, weight_sems,
):
    core = lax.axis_index("dp")
    half = one_ref.shape[1]
    steps, rows = wide.shape[1], wide.shape[3]
    outs = (master_ref, moment_ref, second_ref)

    def store(a, k):
        return pltpu.make_async_copy(
            wide.at[a, k], outs[a].at[:, pl.ds(k * rows, rows)], sems.at[a, k]
        )

    def weights(n, k):
        side = core if n == 0 else 1 - core
        return pltpu.make_async_copy(
            narrow.at[n, k],
            weight_ref.at[:, pl.ds(side * half + k * rows, rows)],
            weight_sems.at[n, k],
        )

    owned, held = ([flag_ref[pl.ds(n + h, 1)] > 0 for h in range(2)] for n in (0, 2))
    both = flag_ref[pl.ds(4, 1)] > 0
    for k in range(steps):
        window = pl.ds(k * rows, rows)
        for a in range(3):
            for h in range(2):
                columns = pl.ds(h * LANES, LANES)
                one = one_ref[a, window, columns].astype(jnp.float32)
                two = two_ref[k, h, a].reshape(rows, LANES).astype(jnp.float32)
                pick = jnp.where(both, two, one)
                wide[a, k, 0, :, columns] = jnp.where(owned[0], one, 0.0)
                wide[a, k, 1, :, columns] = jnp.where(owned[1], pick, 0.0)
                if a == 0:
                    narrow[0, k, 0, :, columns] = jnp.where(held[0], one, 0.0).astype(jnp.bfloat16)
                    narrow[0, k, 1, :, columns] = jnp.where(held[1], pick, 0.0).astype(jnp.bfloat16)
            store(a, k).start()
            if a == 0:
                weights(0, k).start()
        for h in range(2):
            columns = pl.ds(h * LANES, LANES)
            one = other_one_ref[window, columns].astype(jnp.float32)
            two = other_two_ref[k, h].reshape(rows, LANES).astype(jnp.float32)
            pick = jnp.where(both, two, one)
            narrow[1, k, 0, :, columns] = jnp.where(held[0], one, 0.0).astype(jnp.bfloat16)
            narrow[1, k, 1, :, columns] = jnp.where(held[1], pick, 0.0).astype(jnp.bfloat16)
        weights(1, k).start()
    for k in range(steps):
        for a in range(3):
            store(a, k).wait()
        for n in range(2):
            weights(n, k).wait()


def in_hbm(*arrays):
    return [pltpu.with_memory_space_constraint(a, pltpu.HBM) for a in arrays]


def short_exchange(
    keep,
    master_old, moment_old, second_old, grad_parts, old_expert, slot_expert, owner_slot, token_count
):
    half, width = master_old.shape[1:]
    rows = PEERS * PIECE
    chunks = half // rows
    anywhere = pl.BlockSpec(memory_space=pl.ANY)
    vmem = pl.BlockSpec(memory_space=pltpu.VMEM)
    bf16 = jnp.bfloat16
    dma = pltpu.SemaphoreType.DMA
    piece = (PIECE, LANES)
    smem = lambda *shape: pltpu.SMEM(shape, jnp.int32)
    delivered = pl.pallas_call(
        functools.partial(short_kernel, chunks, keep),
        out_shape=(
            pltpu.VMEM((3, half, width), bf16),
            pltpu.VMEM((chunks, 2, 3, SIDE, SIDE, *piece), bf16),
            pltpu.VMEM((half, width), bf16),
            pltpu.VMEM((chunks, 2, SIDE, SIDE, *piece), bf16),
            pltpu.VMEM((8, LANES), jnp.int32),
        ),
        in_specs=[anywhere] * 8,
        out_specs=(vmem,) * 5,
        scratch_shapes=[pltpu.VMEM((PEERS * SPREAD + SIDE * keep, 2, *piece), bf16)] * chunks
        + [pltpu.VMEM((2, SIDE, SIDE, *piece), bf16)] * chunks
        + [pltpu.VMEM((2, SIDE, keep, 3, *piece), bf16)] * chunks
        + [
            pltpu.VMEM((chunks, 3, rows, width), jnp.float32),
            pltpu.VMEM((chunks, 2, rows, width), bf16),
            pltpu.VMEM((chunks, 2, rows, width), bf16),
            pltpu.VMEM((chunks, PEERS, SPREAD, 2, *piece), bf16),
            pltpu.VMEM((chunks, 2, SIDE, SIDE, *piece), bf16),
            pltpu.VMEM((chunks, 2, SIDE, keep, *piece), bf16),
            pltpu.VMEM((chunks, PEERS, 3, PIECE, width), bf16),
            pltpu.VMEM((chunks, 2, SIDE * keep, 3, *piece), bf16),
            pltpu.VMEM((chunks, 2, SIDE, 3, SIDE, *piece), bf16),
            smem(PEERS),
            smem(2 * PEERS),
            smem(PEERS),
            smem(PEERS),
            smem(PEERS),
            smem(2, PEERS),
            smem(2, 2 * PEERS),
            smem(2, SIDE * keep),
            smem(7, PEERS + 2 * SIDE * keep),
            dma((4,)),
            dma((chunks, 4)),
            dma((chunks,)),
            dma((chunks,)),
            dma((chunks,)),
            dma((chunks,)),
            dma((4, chunks)),
            dma((5, chunks)),
            dma((chunks,)),
            dma((chunks, 2)),
            dma((chunks, 2)),
            dma((chunks, 2)),
        ],
        compiler_params=pltpu.CompilerParams(
            collective_id=keep, has_side_effects=True, vmem_limit_bytes=40 << 20
        ),
        name=f"short_exchange_{keep}",
    )(
        *in_hbm(
            old_expert, slot_expert, owner_slot, token_count,
            master_old, moment_old, second_old, grad_parts,
        )
    )
    wide = jax.ShapeDtypeStruct((2, half, width), jnp.float32)
    return pl.pallas_call(
        short_expand_kernel,
        out_shape=(wide, wide, wide, jax.ShapeDtypeStruct((2, 2 * half, width), bf16)),
        in_specs=[vmem] * 5,
        out_specs=(anywhere,) * 4,
        scratch_shapes=[
            pltpu.VMEM((3, chunks, 2, rows, width), jnp.float32),
            pltpu.VMEM((2, chunks, 2, rows, width), bf16),
            dma((3, chunks)),
            dma((2, chunks)),
        ],
        compiler_params=pltpu.CompilerParams(vmem_limit_bytes=24 << 20),
        name=f"short_expand_{keep}",
    )(*delivered)


def short_kernel_allowed(slot_hbm, ok_ref, slot_ref, sem):
    copy = pltpu.make_async_copy(slot_hbm, slot_ref, sem)
    copy.start()
    copy.wait()
    both = [
        jnp.where((slot_ref[2 * d] >= 0) & (slot_ref[2 * d + 1] >= 0), 1, 0) for d in range(PEERS)
    ]
    most = jnp.int32(0)
    for h in range(2):
        for p in range(SIDE):
            line = [both[line_device(h, p, q)] for q in range(SIDE)]
            most = jnp.maximum(most, line[0] + line[1] + line[2] + line[3])
    for n in range(2):
        ok_ref[n] = jnp.where(most <= 2 + n, 1, 0)


def per_device(*args):
    slot_expert = args[5]
    allowed = pl.pallas_call(
        short_kernel_allowed,
        out_shape=jax.ShapeDtypeStruct((2,), jnp.int32),
        in_specs=[pl.BlockSpec(memory_space=pl.ANY)],
        out_specs=pl.BlockSpec(memory_space=pltpu.SMEM),
        scratch_shapes=[pltpu.SMEM(slot_expert.shape, jnp.int32), pltpu.SemaphoreType.DMA],
        name="allowed",
    )(*in_hbm(slot_expert))

    def crowded(*inner):
        return lax.cond(
            allowed[1] > 0, functools.partial(short_exchange, 3), full_exchange, *inner
        )

    return lax.cond(allowed[0] > 0, functools.partial(short_exchange, 2), crowded, *args)


def solution(mesh):
    placed = (
        P("expert", "dp", "etp"),
        P("expert", "dp", "etp"),
        P("expert", "dp", "etp"),
        P("dp", "expert", None, "etp"),
        P(),
        P(),
        P(),
        P(),
    )
    return jax.shard_map(
        per_device,
        mesh=mesh,
        in_specs=placed,
        out_specs=(
            P("expert", "dp", "etp"),
            P("expert", "dp", "etp"),
            P("expert", "dp", "etp"),
            P("expert", None, "etp"),
        ),
        check_vma=False,
    )
```
